32 devices in a mesh: dp: 8 (over y, x, core), narrow: 4 (over z).
Axes of the slice: x: 2, y: 2, z: 4, core: 2. Of those that a mesh axis runs over, the one named last changes fastest.
Arguments:
- tokens: bfloat16 [4, 8, 512, 768], P('narrow', 'dp'), may hold values from -6 to 6
- cotangent: bfloat16 [4, 8, 512, 768], P('narrow', 'dp'), may hold values from -6 to 6
- resets: int32 [4, 8], P(None, 'dp'), may hold values 0 or 1
- truncation: int32 [4], replicated, may hold values from 1 to 8
- memory_state: float32 [4, 768, 2304], P(None, None, 'narrow'), may hold values from -192 to 192
- normalizer: float32 [4, 2304], P(None, 'narrow'), may hold values from 0.5 to 2
- query_weight: bfloat16 [768, 384], P(('dp', 'narrow')), may hold values from -0.21875 to 0.21875
- key_weight: bfloat16 [768, 384], P(('dp', 'narrow')), may hold values from -0.21875 to 0.21875
- value_weight: bfloat16 [768, 768], P(('dp', 'narrow')), may hold values from -1.75 to 1.75
- gate_weight: bfloat16 [768], P(('dp', 'narrow')), may hold values from -0.21875 to 0.21875
- first_gain: bfloat16 [768], P(('dp', 'narrow')), may hold values from 0.5 to 1.5
- mixing_weight: bfloat16 [768, 2304], P(('dp', 'narrow')), may hold values from -0.21875 to 0.21875
- output_weight: bfloat16 [768, 768], P(('dp', 'narrow')), may hold values from -0.875 to 0.875
- second_gain: bfloat16 [768], P(('dp', 'narrow')), may hold values from 0.5 to 1.5
- expand_weight: bfloat16 [768, 3072], P(('dp', 'narrow')), may hold values from -0.21875 to 0.21875
- reduce_weight: bfloat16 [3072, 768], P(('dp', 'narrow')), may hold values from -0.109375 to 0.109375
Outputs:
- block_out: bfloat16 [4, 8, 512, 768], P('narrow', 'dp')
- token_grad: float32 [4, 8, 512, 768], P('narrow', 'dp')
- query_grad: float32 [768, 384], P(('dp', 'narrow'))
- key_grad: float32 [768, 384], P(('dp', 'narrow'))
- value_grad: float32 [768, 768], P(('dp', 'narrow'))
- gate_grad: float32 [768], P(('dp', 'narrow'))
- first_grad: float32 [768], P(('dp', 'narrow'))
- mixing_grad: float32 [768, 2304], P(('dp', 'narrow'))
- output_grad: float32 [768, 768], P(('dp', 'narrow'))
- second_grad: float32 [768], P(('dp', 'narrow'))
- expand_grad: float32 [768, 3072], P(('dp', 'narrow'))
- reduce_grad: float32 [3072, 768], P(('dp', 'narrow'))
The draws below stay inside these ranges and needn't reach their ends.
Inputs may be any that keep to these rules, and one draw needn't show every extreme that they name: `resets`: 1 marks a segment that begins a new document: its memory read ignores everything written before it. Gradients reach the memory writes of the last truncation[s] segments of stream s only.
All inputs are finite; a program needn't handle non-finite values. No bound on the sum of `resets` on one device may be relied on, other than what follows from the above.
Results may differ from the reference program's by a relative error of at most 0.02.
Values may be sent and summed in bfloat16 or wider, within the bound.
A program may use at most 512 MiB of HBM per device.

```python
from functools import partial
import jax
import jax.numpy as jnp
from jax import lax

D = 768
HEADS = 12
HD = 64
FF = 3072
KD = 384
NU = 3
MEM = 16
L = 512
F = 2304
STREAMS = 4
NSEG = 8


def plant(values, stream_key, smallest, top_value):
    longest = values.shape.index(max(values.shape))
    spots = []
    for shift in (0, 1):
        where = [jax.random.randint(jax.random.fold_in(stream_key, axis), (), 0, length) for axis, length in enumerate(values.shape)]
        where[longest] = (where[longest] + shift) % values.shape[longest]
        spots.append(tuple(where))
    return values.at[spots[0]].set(smallest).at[spots[1]].set(top_value)


def block_levels(key, dims, split, low, top_value):
    def one(dim, shards_of):
        heights = jax.random.uniform(jax.random.fold_in(jax.random.fold_in(key, 6), dim), (shards_of,), jnp.float32, low / len(split), top_value / len(split))
        return jnp.repeat(jnp.exp(heights), dims[dim] // shards_of).reshape((-1,) + (1,) * (len(dims) - dim - 1))

    loudness = one(*split[0])
    for cut in split[1:]:
        loudness = loudness * one(*cut)
    return loudness


def bell_draw(stream_key, shape, scale, limit, split=(), held_as=jnp.bfloat16):
    entries = jax.random.normal(stream_key, shape, jnp.float32) * scale
    if len(split) > 0:
        entries = block_levels(stream_key, shape, split, -0.22, 0.18) * entries
    return jnp.clip(entries, min=-limit, max=limit).astype(held_as)


def setup_inputs(seed: int = 0) -> dict:
    splits = jax.random.split(jax.random.key(seed), 17)
    tokens = bell_draw(splits[0], (STREAMS, NSEG, L, D), 1.0, 6.0, ((0, 4), (1, 8)))
    cotangent = bell_draw(splits[1], (STREAMS, NSEG, L, D), 1.0, 6.0, ((0, 4), (1, 8)))
    resets = plant((jax.random.randint(splits[2], (STREAMS, NSEG), 0, 6) < 1).astype(jnp.int32), jax.random.fold_in(splits[2], 1), 0, 1)
    truncation = plant(jax.random.randint(splits[3], (STREAMS,), 1, NSEG + 1), jax.random.fold_in(splits[3], 1), 1, NSEG).astype(jnp.int32)
    memory_state = bell_draw(splits[4], (STREAMS, D, F), 32.0, 192.0, ((2, 4),), jnp.float32)
    normalizer = jnp.clip(0.5 + 1.5 * jax.random.uniform(splits[5], (STREAMS, F), jnp.float32) ** block_levels(splits[5], (STREAMS, F), ((1, 4),), -0.2, 0.2), 0.5, 2.0)
    query_weight = bell_draw(splits[6], (D, KD), D ** -0.5, 0.21875, ((0, 32),))
    key_weight = bell_draw(splits[7], (D, KD), D ** -0.5, 0.21875, ((0, 32),))
    value_weight = bell_draw(splits[8], (D, D), (D // 64) ** -0.5, 1.75, ((0, 32),))
    gate_weight = bell_draw(splits[9], (D,), D ** -0.5, 0.21875, ((0, 32),))
    first_gain = jnp.clip(1.0 + 0.1 * jax.random.normal(splits[10], (D,), jnp.float32), 0.5, 1.5).astype(jnp.bfloat16)
    mixing_weight = bell_draw(splits[11], (D, 3 * D), D ** -0.5, 0.21875, ((0, 32),))
    output_weight = bell_draw(splits[12], (D, D), (D // 16) ** -0.5, 0.875, ((0, 32),))
    second_gain = jnp.clip(1.0 + 0.1 * jax.random.normal(splits[13], (D,), jnp.float32), 0.5, 1.5).astype(jnp.bfloat16)
    expand_weight = bell_draw(splits[14], (D, FF), D ** -0.5, 0.21875, ((0, 32),))
    reduce_weight = bell_draw(splits[15], (FF, D), FF ** -0.5, 0.109375, ((0, 32),))
    return {"tokens": tokens, "cotangent": cotangent, "resets": resets, "truncation": truncation, "memory_state": memory_state, "normalizer": normalizer, "query_weight": query_weight, "key_weight": key_weight, "value_weight": value_weight, "gate_weight": gate_weight, "first_gain": first_gain, "mixing_weight": mixing_weight, "output_weight": output_weight, "second_gain": second_gain, "expand_weight": expand_weight, "reduce_weight": reduce_weight}


@jax.custom_vjp
def low(v):
    return lax.optimization_barrier(v.astype(jnp.bfloat16)).astype(jnp.float32)

@jax.custom_vjp
def low_back(v):
    return v

def low_keep(v):
    return (low(v), None)

def low_pass(kept, grad):
    return (grad,)

def back_keep(v):
    return (v, None)

def back_low(kept, grad):
    return (low(grad),)
low.defvjp(low_keep, low_pass)
low_back.defvjp(back_keep, back_low)
exact_mode = lax.Precision.HIGHEST
ln_eps = 1e-05
masked_score = -1e+30

def product(left, right):
    return jnp.dot(left, right, precision=exact_mode)

def features(inputs):
    halves = jnp.concatenate([jax.nn.relu(inputs), jax.nn.relu(-inputs)], axis=-1)
    return jnp.concatenate([halves * jnp.roll(halves, offset, axis=-1) for offset in range(1, NU + 1)], axis=-1)

def layer_norm(inputs, gain):
    center = inputs - lax.optimization_barrier(jnp.mean(inputs, axis=-1, keepdims=True))
    spread = lax.optimization_barrier(jnp.mean(center * center, axis=-1, keepdims=True))
    return center * lax.rsqrt(spread + ln_eps) * gain

def write_rows(tokens_in, key_w, value_w, gate_w):
    memory_rows = tokens_in[:, :, L - MEM:, :]
    write_keys = low_back(low(jnp.einsum('abmd,dk->abmk', memory_rows, key_w, precision=exact_mode)))
    write_vals = low_back(low(jnp.einsum('abmd,de->abme', memory_rows, value_w, precision=exact_mode)))
    gate_logit = jnp.einsum('abmd,d->abm', memory_rows, gate_w, precision=exact_mode)
    gate_prob = low_back(low(jax.nn.sigmoid(gate_logit)))
    return (write_keys, write_vals, gate_prob)

def segment_step(weights, carry, inputs):
    query_w, gain_one, mixing_w, output_w, gain_two, expand_w, reduce_w = weights
    memory_now, normal_now = carry
    seg_tokens, write_keys, write_vals, gate_prob, keep_flag = inputs
    memory_read = keep_flag * memory_now
    normal_read = keep_flag * normal_now
    mem_query = low_back(low(product(seg_tokens, query_w)))
    query_features = low(features(mem_query))
    numerator = low_back(product(query_features, low(memory_read).T))
    den_sum = low_back(product(query_features, normal_read))
    first_res = seg_tokens + numerator / (1.0 + den_sum)[:, None]
    normed_one = low(layer_norm(first_res, gain_one))
    mixed = product(normed_one, mixing_w)
    queries = low_back(low(mixed[:, :D])).reshape(L, HEADS, HD)
    key_all = low_back(low(mixed[:, D:2 * D])).reshape(L, HEADS, HD)
    values = low_back(low(mixed[:, 2 * D:])).reshape(L, HEADS, HD)
    scores = low_back(jnp.einsum('qhd,khd->hqk', queries, key_all, precision=exact_mode) * HD ** (-0.5))
    position = jnp.arange(L)
    causal = position[None, :] <= position[:, None]
    scores = jnp.where(causal[None], scores, masked_score)
    probs = jax.nn.softmax(scores, axis=-1)
    attended = jnp.einsum('hqk,khd->qhd', low(probs), values, precision=exact_mode).reshape(L, D)
    attended = low_back(low(attended))
    branch = low_back(product(attended, output_w))
    second_res = first_res + branch
    normed_two = low(layer_norm(second_res, gain_two))
    expanded = low_back(product(normed_two, expand_w))
    activated = low(jax.nn.gelu(expanded, approximate=True))
    reduced = low_back(product(activated, reduce_w))
    block = second_res + reduced
    key_feat = low(features(write_keys))
    scaled_vals = write_vals * gate_prob[:, None]
    memory_next = memory_read + product(scaled_vals.T, key_feat)
    normal_next = normal_read + lax.optimization_barrier(jnp.sum(key_feat, axis=0))
    return ((memory_next, normal_next), block)

def reference(tokens, cotangent, resets, truncation, memory_state, normalizer, query_weight, key_weight, value_weight, gate_weight, first_gain, mixing_weight, output_weight, second_gain, expand_weight, reduce_weight):
    params = [matrix.astype(jnp.float32) for matrix in (query_weight, key_weight, value_weight, gate_weight, first_gain, mixing_weight, output_weight, second_gain, expand_weight, reduce_weight)]
    tokens_f = tokens.astype(jnp.float32)
    keep_flags = 1.0 - resets.astype(jnp.float32)
    live = jnp.arange(NSEG, dtype=jnp.int32)[None, :] >= (NSEG - truncation)[:, None]
    fixed_keys, fixed_vals, fixed_gates = write_rows(tokens_f, params[1], params[2], params[3])
    memory_f = memory_state.astype(jnp.float32)
    normal_f = normalizer.astype(jnp.float32)

    def forward(tokens_in, query_w, key_w, value_w, gate_w, gain_one, mixing_w, output_w, gain_two, expand_w, reduce_w):
        fresh_keys, fresh_vals, fresh_gates = write_rows(tokens_in, key_w, value_w, gate_w)
        use_keys = jnp.where(live[:, :, None, None], fresh_keys, fixed_keys)
        use_vals = jnp.where(live[:, :, None, None], fresh_vals, fixed_vals)
        use_gates = jnp.where(live[:, :, None], fresh_gates, fixed_gates)
        weights = (query_w, gain_one, mixing_w, output_w, gain_two, expand_w, reduce_w)
        step_fn = jax.checkpoint(partial(segment_step, weights))

        def one_stream(stream_in):
            seg_tokens, wkeys, wvals, gates, keeps, mem_start, norm_start = stream_in
            final_state, blocks = lax.scan(step_fn, (mem_start, norm_start), (seg_tokens, wkeys, wvals, gates, keeps))
            return blocks
        return lax.map(one_stream, (tokens_in, use_keys, use_vals, use_gates, keep_flags, memory_f, normal_f))
    block_out, pullback = jax.vjp(forward, tokens_f, *params)
    grads = pullback(cotangent.astype(jnp.float32))
    return (block_out.astype(jnp.bfloat16), grads[0], grads[1], grads[2], grads[3], grads[4], grads[5], grads[6], grads[7], grads[8], grads[9], grads[10])
```

```python
import jax
import jax.numpy as jnp
from jax import lax
from jax.sharding import PartitionSpec as P

HEADS = 12
HD = 64
MEM = 16
ORDER = 3


exact_mode = lax.Precision.HIGHEST
ln_eps = 1e-05
masked_score = -1e30
bf_type = jnp.bfloat16
float_kind = jnp.float32


def matmul(left, right):
    return jnp.dot(left, right, preferred_element_type=float_kind)


def rounded(values):
    return lax.optimization_barrier(values.astype(bf_type)).astype(float_kind)


def halves_of(inputs):
    return jnp.concatenate([jax.nn.relu(inputs), jax.nn.relu(-inputs)], axis=-1)


def features(inputs):
    halves = halves_of(inputs)
    return jnp.concatenate(
        [halves * jnp.roll(halves, shift, axis=-1) for shift in range(1, ORDER + 1)], axis=-1
    )


def features_back(inputs, grad):
    key_width = inputs.shape[-1]
    halves = halves_of(inputs)
    total = jnp.zeros_like(halves)
    for shift in range(1, ORDER + 1):
        part = grad[:, (shift - 1) * 2 * key_width : shift * 2 * key_width]
        total = total + part * jnp.roll(halves, shift, axis=-1)
        total = total + jnp.roll(part * halves, -shift, axis=-1)
    return jnp.where(inputs > 0, total[:, :key_width], 0.0) - jnp.where(
        inputs < 0, total[:, key_width:], 0.0
    )


def exact(left, right):
    return jnp.dot(left, right, precision=exact_mode)


def norm_forward(inputs, gain):
    center = inputs - jnp.mean(inputs, axis=-1, keepdims=True)
    inv_std = lax.rsqrt(jnp.mean(center * center, axis=-1, keepdims=True) + ln_eps)
    unit = center * inv_std
    return (unit * gain, unit, inv_std)


def norm_backward(grad_out, unit, inv_std, gain):
    grad_unit = grad_out * gain
    grad_gain = jnp.sum(grad_out * unit, axis=0)
    grad_in = inv_std * (
        grad_unit
        - jnp.mean(grad_unit, axis=-1, keepdims=True)
        - unit * jnp.mean(grad_unit * unit, axis=-1, keepdims=True)
    )
    return (grad_in, grad_gain)


def block_scores(query_blk, key_seg, row_start):
    raw = jnp.einsum(
        "qhd,khd->hqk", query_blk, key_seg, preferred_element_type=float_kind
    ) * query_blk.shape[-1] ** (-0.5)
    rows_pos = row_start + jnp.arange(query_blk.shape[0])
    cols_pos = jnp.arange(key_seg.shape[0])
    return jnp.where((cols_pos[None, :] <= rows_pos[:, None])[None], raw, masked_score)


def body(
    tokens,
    cotangent,
    resets,
    truncation,
    memory_state,
    normalizer,
    query_weight,
    key_weight,
    value_weight,
    gate_weight,
    first_gain,
    mixing_weight,
    output_weight,
    second_gain,
    expand_weight,
    reduce_weight,
):
    query_w, key_w, value_w, gate_w, gain_one, mixing_w, output_w, gain_two, expand_w, reduce_w = (
        lax.all_gather(query_weight, ("dp", "narrow"), axis=0, tiled=True),
        lax.all_gather(key_weight, ("dp", "narrow"), axis=0, tiled=True),
        lax.all_gather(value_weight, ("dp", "narrow"), axis=0, tiled=True),
        lax.all_gather(gate_weight, ("dp", "narrow"), axis=0, tiled=True),
        lax.all_gather(first_gain, ("dp", "narrow"), axis=0, tiled=True),
        lax.all_gather(mixing_weight, ("dp", "narrow"), axis=0, tiled=True),
        lax.all_gather(output_weight, ("dp", "narrow"), axis=0, tiled=True),
        lax.all_gather(second_gain, ("dp", "narrow"), axis=0, tiled=True),
        lax.all_gather(expand_weight, ("dp", "narrow"), axis=0, tiled=True),
        lax.all_gather(reduce_weight, ("dp", "narrow"), axis=0, tiled=True),
    )
    seg_count = tokens.shape[0]
    seg_len = tokens.shape[2]
    width = tokens.shape[3]
    row_count = seg_count * seg_len
    key_width = query_w.shape[1]
    stream_count = memory_state.shape[0]
    gain_one_f = gain_one.astype(float_kind)
    gain_two_f = gain_two.astype(float_kind)
    tok_rows = tokens.reshape(row_count, width)
    memory_rows = tokens[:, 0, seg_len - MEM :, :].reshape(seg_count * MEM, width)
    mem_query = matmul(tok_rows, query_w).astype(bf_type)
    write_keys = matmul(memory_rows, key_w).astype(bf_type)
    write_vals = matmul(memory_rows, value_w).astype(bf_type)
    gate_prob = jax.nn.sigmoid(matmul(memory_rows, gate_w))
    gate_low = gate_prob.astype(bf_type)
    place = lax.axis_index("dp")
    places = lax.axis_size("dp")
    stream = lax.axis_index("narrow")
    keep_flag = 1.0 - resets.astype(float_kind)
    own_keep = lax.dynamic_index_in_dim(keep_flag[:, 0], stream, 0, False)
    packed = jnp.concatenate(
        [
            write_keys,
            write_vals,
            jnp.broadcast_to(gate_low[:, None], (MEM, 64)),
            jnp.broadcast_to(own_keep.astype(bf_type), (MEM, 64)),
        ],
        axis=1,
    )
    all_rows = lax.all_gather(packed, "dp", axis=0, tiled=True).astype(float_kind)
    all_keys = all_rows[:, :key_width]
    all_vals = all_rows[:, key_width : key_width + width]
    all_gates = all_rows[:, key_width + width : key_width + width + 1]
    keeps = all_rows[::MEM, key_width + width + 64]
    index = jnp.arange(places)
    linked = jnp.prod(
        jnp.where(
            (index[None, :] > index[:, None]) & (index[None, :] <= place), keeps[None, :], 1.0
        ),
        axis=1,
    ) * (index < place)
    start_keep = jnp.prod(jnp.where(index <= place, keeps, 1.0))
    row_link = jnp.repeat(linked, MEM)[None, :]
    key_feat = features(all_keys).astype(bf_type)
    scaled_vals = all_vals * all_gates
    memory_parts = lax.all_to_all(memory_state.astype(bf_type), "narrow", 0, 0, tiled=True)
    memory_own = jnp.concatenate(
        [memory_parts[i] for i in range(stream_count)], axis=-1
    )
    normal_all = lax.all_gather(normalizer, "narrow", axis=1, tiled=True)
    normal_own = lax.dynamic_index_in_dim(normal_all, stream, 0, False)
    query_features = features(mem_query.astype(float_kind)).astype(bf_type)
    row_scores = (
        lax.dot_general(
            query_features, key_feat, (((1,), (1,)), ((), ())), preferred_element_type=float_kind
        )
        * row_link
    )
    numerator = start_keep * lax.dot_general(
        query_features, memory_own, (((1,), (1,)), ((), ())), preferred_element_type=float_kind
    ) + exact(row_scores, scaled_vals)
    den_sum = start_keep * jnp.sum(
        query_features.astype(float_kind) * normal_own[None, :], axis=1
    ) + jnp.sum(row_scores, axis=1)
    den_total = 1.0 + den_sum
    first_res = tok_rows.astype(float_kind) + numerator / den_total[:, None]
    normed_one, unit_one, inv_one = norm_forward(first_res, gain_one_f)
    normed_one_low = normed_one.astype(bf_type)
    mixed = matmul(normed_one_low, mixing_w)
    queries = mixed[:, :width].astype(bf_type).reshape(seg_count, seg_len, HEADS, HD)
    key_heads = mixed[:, width : 2 * width].astype(bf_type).reshape(seg_count, seg_len, HEADS, HD)
    head_values = mixed[:, 2 * width :].astype(bf_type).reshape(seg_count, seg_len, HEADS, HD)
    block_rows = min(seg_len, 512)
    block_count = seg_len // block_rows

    def attend(flat_idx):
        seg_idx = flat_idx // block_count
        row_start = flat_idx % block_count * block_rows
        query_seg = lax.dynamic_index_in_dim(queries, seg_idx, 0, keepdims=False)
        key_seg = lax.dynamic_index_in_dim(key_heads, seg_idx, 0, keepdims=False)
        value_seg = lax.dynamic_index_in_dim(head_values, seg_idx, 0, keepdims=False)
        scores = block_scores(query_seg, key_seg, row_start)
        top_score = jnp.max(scores, axis=-1, keepdims=True)
        raw_weights = jnp.exp(scores - top_score)
        exp_total = jnp.sum(raw_weights, axis=-1, keepdims=True)
        log_total = top_score[..., 0] + jnp.log(exp_total[..., 0])
        probs = (raw_weights / exp_total).astype(bf_type)
        attended_blk = jnp.einsum(
            "hqk,khd->qhd", probs, value_seg, preferred_element_type=float_kind
        ).astype(bf_type)
        return (attended_blk, log_total)

    attended, log_totals = lax.map(attend, jnp.arange(seg_count * block_count, dtype=jnp.int32))
    attended_rows = attended.reshape(row_count, width)
    log_totals = log_totals.reshape(seg_count, block_count, HEADS, block_rows)
    branch = matmul(attended_rows, output_w)
    second_res = first_res + branch
    normed_two, unit_two, inv_two = norm_forward(second_res, gain_two_f)
    normed_two_low = normed_two.astype(bf_type)
    expanded = matmul(normed_two_low, expand_w)
    activated_low = jax.nn.gelu(expanded, approximate=True).astype(bf_type)
    reduced = matmul(activated_low, reduce_w)
    block_out = (second_res + reduced).astype(bf_type).reshape(seg_count, 1, seg_len, width)
    grad_block = cotangent.reshape(row_count, width)
    grad_reduce = matmul(activated_low.T, grad_block)
    grad_act = matmul(grad_block, reduce_w.T)
    unused, gelu_pull = jax.vjp(lambda inputs: jax.nn.gelu(inputs, approximate=True), expanded)
    grad_expanded = gelu_pull(grad_act)[0].astype(bf_type)
    grad_expand = matmul(normed_two_low.T, grad_expanded)
    grad_normed_two = matmul(grad_expanded, expand_w.T)
    grad_in_two, grad_gain_two = norm_backward(grad_normed_two, unit_two, inv_two, gain_two_f)
    grad_second = grad_block.astype(float_kind) + grad_in_two
    grad_branch = grad_second.astype(bf_type)
    grad_output = matmul(attended_rows.T, grad_branch)
    grad_att = (
        matmul(grad_branch, output_w.T).astype(bf_type).reshape(seg_count, seg_len, HEADS, HD)
    )

    def attend_back(items):
        query_seg, key_seg, value_seg, grad_seg, log_seg = items
        score_scale = query_seg.shape[-1] ** (-0.5)
        scores = block_scores(query_seg, key_seg, 0)
        probs = jnp.exp(scores - log_seg[0][:, :, None])
        grad_value = jnp.einsum(
            "hqk,qhd->khd", probs.astype(bf_type), grad_seg, preferred_element_type=float_kind
        )
        grad_probs = jnp.einsum(
            "qhd,khd->hqk", grad_seg, value_seg, preferred_element_type=float_kind
        )
        grad_scores = (
            probs * (grad_probs - jnp.sum(probs * grad_probs, axis=-1, keepdims=True))
        ).astype(bf_type)
        query_parts = [
            (
                jnp.einsum("hqk,khd->qhd", grad_scores, key_seg, preferred_element_type=float_kind)
                * score_scale
            ).astype(bf_type)
        ]
        grad_key = (
            jnp.einsum("hqk,qhd->khd", grad_scores, query_seg, preferred_element_type=float_kind)
            * score_scale
        )
        return (
            jnp.concatenate(query_parts, axis=0),
            grad_key.astype(bf_type),
            grad_value.astype(bf_type),
        )

    grad_queries, grad_keys, grad_values = lax.map(
        attend_back, (queries, key_heads, head_values, grad_att, log_totals)
    )
    grad_mixed = jnp.concatenate(
        [
            grad_queries.reshape(row_count, width),
            grad_keys.reshape(row_count, width),
            grad_values.reshape(row_count, width),
        ],
        axis=1,
    )
    grad_mixing = matmul(normed_one_low.T, grad_mixed)
    grad_normed_one = matmul(grad_mixed, mixing_w.T)
    grad_in_one, grad_gain_one = norm_backward(grad_normed_one, unit_one, inv_one, gain_one_f)
    grad_first = grad_second + grad_in_one
    grad_num = (grad_first / den_total[:, None]).astype(bf_type)
    grad_den = (-jnp.sum(grad_first * numerator, axis=-1) / (den_total * den_total)).astype(bf_type)
    grad_num_f = grad_num.astype(float_kind)
    grad_den_f = grad_den.astype(float_kind)[:, None]
    grad_scores_mem = (exact(grad_num_f, scaled_vals.T) + grad_den_f) * row_link
    grad_feat = start_keep * (
        matmul(grad_num, memory_own) + grad_den_f * normal_own[None, :]
    ) + exact(grad_scores_mem, key_feat.astype(float_kind))
    grad_mq = features_back(mem_query.astype(float_kind), grad_feat)
    grad_key_feat = exact(grad_scores_mem.T, query_features.astype(float_kind))
    grad_rows = jnp.concatenate(
        [features_back(all_keys, grad_key_feat), exact(row_scores.T, grad_num_f)], axis=1
    )
    live = (place >= places - lax.dynamic_index_in_dim(truncation, stream, 0, False)).astype(
        float_kind
    )
    own_rows = lax.psum_scatter(grad_rows, "dp", scatter_dimension=0, tiled=True) * live
    grad_wk = own_rows[:, :key_width]
    grad_wv = own_rows[:, key_width:] * gate_low.astype(float_kind)[:, None]
    grad_gate = jnp.sum(own_rows[:, key_width:] * write_vals.astype(float_kind), axis=1)
    grad_mq_low = grad_mq.astype(bf_type)
    grad_wk_low = grad_wk.astype(bf_type)
    grad_wv_low = grad_wv.astype(bf_type)
    grad_logit = grad_gate.astype(bf_type).astype(float_kind) * gate_prob * (1.0 - gate_prob)
    token_rows = grad_first + matmul(grad_mq_low, query_w.T)
    memory_extra = (
        matmul(grad_wk_low, key_w.T)
        + matmul(grad_wv_low, value_w.T)
        + grad_logit[:, None] * gate_w.astype(float_kind)[None, :]
    )
    token_seg = token_rows.reshape(seg_count, seg_len, width)
    token_seg = token_seg.at[:, seg_len - MEM :, :].add(memory_extra.reshape(seg_count, MEM, width))
    token_grad = token_seg.reshape(seg_count, 1, seg_len, width)
    grad_query = matmul(tok_rows.T, grad_mq_low)
    grad_key = matmul(memory_rows.T, grad_wk_low)
    grad_value = matmul(memory_rows.T, grad_wv_low)
    grad_gate_w = jnp.dot(memory_rows.astype(float_kind).T, grad_logit, precision=exact_mode)
    summed = (
        lax.psum_scatter(grad_query, ("dp", "narrow"), scatter_dimension=0, tiled=True),
        lax.psum_scatter(grad_key, ("dp", "narrow"), scatter_dimension=0, tiled=True),
        lax.psum_scatter(grad_value, ("dp", "narrow"), scatter_dimension=0, tiled=True),
        lax.psum_scatter(grad_gate_w, ("dp", "narrow"), scatter_dimension=0, tiled=True),
        lax.psum_scatter(grad_gain_one, ("dp", "narrow"), scatter_dimension=0, tiled=True),
        lax.psum_scatter(grad_mixing, ("dp", "narrow"), scatter_dimension=0, tiled=True),
        lax.psum_scatter(grad_output, ("dp", "narrow"), scatter_dimension=0, tiled=True),
        lax.psum_scatter(grad_gain_two, ("dp", "narrow"), scatter_dimension=0, tiled=True),
        lax.psum_scatter(grad_expand, ("dp", "narrow"), scatter_dimension=0, tiled=True),
        lax.psum_scatter(grad_reduce, ("dp", "narrow"), scatter_dimension=0, tiled=True),
    )
    return (
        block_out,
        token_grad,
        summed[0],
        summed[1],
        summed[2],
        summed[3],
        summed[4],
        summed[5],
        summed[6],
        summed[7],
        summed[8],
        summed[9],
    )


def solution(mesh):
    placed = (
        P("narrow", "dp", None, None),
        P("narrow", "dp", None, None),
        P(None, "dp"),
        P(),
        P(None, None, "narrow"),
        P(None, "narrow"),
        P(("dp", "narrow"), None),
        P(("dp", "narrow"), None),
        P(("dp", "narrow"), None),
        P(("dp", "narrow")),
        P(("dp", "narrow")),
        P(("dp", "narrow"), None),
        P(("dp", "narrow"), None),
        P(("dp", "narrow")),
        P(("dp", "narrow"), None),
        P(("dp", "narrow"), None),
    )
    return jax.shard_map(
        body,
        mesh=mesh,
        in_specs=placed,
        out_specs=(
            P("narrow", "dp", None, None),
            P("narrow", "dp", None, None),
            P(("dp", "narrow"), None),
            P(("dp", "narrow"), None),
            P(("dp", "narrow"), None),
            P(("dp", "narrow")),
            P(("dp", "narrow")),
            P(("dp", "narrow"), None),
            P(("dp", "narrow"), None),
            P(("dp", "narrow")),
            P(("dp", "narrow"), None),
            P(("dp", "narrow"), None),
        ),
        check_vma=False,
    )
```

```python
import jax
import jax.numpy as jnp
from jax import lax
from jax.sharding import PartitionSpec as P

HEADS = 12
HD = 64
MEM = 16
ORDER = 3


exact_mode = lax.Precision.HIGHEST
ln_eps = 1e-05
masked_score = -1e30
bf_type = jnp.bfloat16
float_kind = jnp.float32


def bits_of(axis):
    count = lax.axis_size(axis)
    bit = 1
    out = []
    while bit < count:
        out.append((axis, bit))
        bit *= 2
    return out[::-1]

def place_bits():
    return bits_of("dp") + bits_of("narrow")

def own_bit(spot):
    axis, bit = spot
    return (lax.axis_index(axis) // bit) % 2

def exchange(values, spot):
    axis, bit = spot
    return lax.ppermute(values, axis, [(i, i ^ bit) for i in range(lax.axis_size(axis))])

def gather_bits(shard, order, all_bits):
    held = []
    whole = shard
    for spot in order:
        other = exchange(whole, spot)
        at = sum(all_bits.index(b) < all_bits.index(spot) for b in held)
        low = own_bit(spot) == 0
        whole = jnp.where(low, jnp.stack([whole, other], at), jnp.stack([other, whole], at))
        held.append(spot)
    return whole

def scatter_bits(whole, order, all_bits):
    held = list(all_bits)
    for spot in order:
        at = held.index(spot)
        mine = own_bit(spot)
        other = exchange(lax.dynamic_index_in_dim(whole, 1 - mine, at, False).astype(bf_type), spot)
        whole = lax.dynamic_index_in_dim(whole, mine, at, False).astype(float_kind) + other.astype(float_kind)
        held.remove(spot)
    return whole

def two_orders():
    inner, outer = bits_of("dp")[-1:], bits_of("dp")[:-1]
    return outer + inner, outer[::-1] + inner


def swap_blocks(blocks, spots):
    for at, spot in enumerate(spots):
        mine = own_bit(spot)
        other = exchange(lax.dynamic_index_in_dim(blocks, 1 - mine, at, False), spot)
        kept = lax.dynamic_index_in_dim(blocks, mine, at, False)
        blocks = jnp.where(mine == 0, jnp.stack([kept, other], at), jnp.stack([other, kept], at))
    return blocks


def gather_weight(shard, order):
    whole = gather_bits(shard, bits_of("narrow") + order, place_bits())
    return whole.reshape((-1, shard.shape[-1]))


def scatter_weight(whole, order):
    spots = place_bits()
    split = whole.reshape((2,) * len(spots) + (whole.shape[0] // 2 ** len(spots), whole.shape[1]))
    return scatter_bits(split, order[::-1] + bits_of("narrow")[::-1], spots)


def matmul(left, right):
    return jnp.dot(left, right, preferred_element_type=float_kind)


def rounded(values):
    return lax.optimization_barrier(values.astype(bf_type)).astype(float_kind)


def halves_of(inputs):
    return jnp.concatenate([jax.nn.relu(inputs), jax.nn.relu(-inputs)], axis=-1)


def features(inputs):
    halves = halves_of(inputs)
    return jnp.concatenate(
        [halves * jnp.roll(halves, shift, axis=-1) for shift in range(1, ORDER + 1)], axis=-1
    )


def features_back(inputs, grad):
    key_width = inputs.shape[-1]
    halves = halves_of(inputs)
    total = jnp.zeros_like(halves)
    for shift in range(1, ORDER + 1):
        part = grad[:, (shift - 1) * 2 * key_width : shift * 2 * key_width]
        total = total + part * jnp.roll(halves, shift, axis=-1)
        total = total + jnp.roll(part * halves, -shift, axis=-1)
    return jnp.where(inputs > 0, total[:, :key_width], 0.0) - jnp.where(
        inputs < 0, total[:, key_width:], 0.0
    )


def exact(left, right):
    return jnp.dot(left, right, precision=exact_mode)


def norm_forward(inputs, gain):
    center = inputs - jnp.mean(inputs, axis=-1, keepdims=True)
    inv_std = lax.rsqrt(jnp.mean(center * center, axis=-1, keepdims=True) + ln_eps)
    unit = center * inv_std
    return (unit * gain, unit, inv_std)


def norm_backward(grad_out, unit, inv_std, gain):
    grad_unit = grad_out * gain
    grad_gain = jnp.sum(grad_out * unit, axis=0)
    grad_in = inv_std * (
        grad_unit
        - jnp.mean(grad_unit, axis=-1, keepdims=True)
        - unit * jnp.mean(grad_unit * unit, axis=-1, keepdims=True)
    )
    return (grad_in, grad_gain)


def block_scores(query_blk, key_seg, row_start):
    raw = jnp.einsum(
        "qhd,khd->hqk", query_blk, key_seg, preferred_element_type=float_kind
    ) * query_blk.shape[-1] ** (-0.5)
    rows_pos = row_start + jnp.arange(query_blk.shape[0])
    cols_pos = jnp.arange(key_seg.shape[0])
    return jnp.where((cols_pos[None, :] <= rows_pos[:, None])[None], raw, masked_score)


def body(
    tokens,
    cotangent,
    resets,
    truncation,
    memory_state,
    normalizer,
    query_weight,
    key_weight,
    value_weight,
    gate_weight,
    first_gain,
    mixing_weight,
    output_weight,
    second_gain,
    expand_weight,
    reduce_weight,
):
    order_a, order_b = two_orders()
    narrow_bits = bits_of("narrow")
    dp_bits = bits_of("dp")
    key_width = query_weight.shape[1]
    width = tokens.shape[3]
    vectors = jnp.stack([gate_weight, first_gain, second_gain], axis=1)
    early_b = gather_weight(
        jnp.concatenate(
            [query_weight, key_weight, jnp.pad(vectors, ((0, 0), (0, 125)))], axis=1
        ),
        order_b,
    )
    value_w = gather_weight(value_weight, order_a)
    query_w = early_b[:, :key_width]
    key_w = early_b[:, key_width : 2 * key_width]
    gate_w = early_b[:, 2 * key_width]
    gain_one = early_b[:, 2 * key_width + 1]
    gain_two = early_b[:, 2 * key_width + 2]
    stream_count = memory_state.shape[0]
    memory_halves = []
    block_rows = width // lax.axis_size("dp") // 2
    for half, order in enumerate((order_a, order_b)):
        rows = lax.dynamic_slice_in_dim(
            memory_state, half * (width // 2) + lax.axis_index("dp") * block_rows, block_rows, 1
        ).astype(bf_type)
        split = rows.reshape((2,) * len(narrow_bits) + rows.shape[1:])
        swapped = swap_blocks(split, narrow_bits).reshape(rows.shape)
        wide = jnp.concatenate([swapped[i] for i in range(stream_count)], axis=-1)
        memory_halves.append(
            gather_bits(wide, order, dp_bits).reshape((width // 2, wide.shape[-1]))
        )
    memory_top, memory_low = memory_halves
    normal_split = normalizer.reshape((2,) * len(narrow_bits) + normalizer.shape[1:])
    normal_own = swap_blocks(normal_split, narrow_bits).reshape(-1)
    mixing_a = gather_weight(mixing_weight[:, : 2 * width], order_a)
    middle_b = gather_weight(
        jnp.concatenate([mixing_weight[:, 2 * width :], output_weight], axis=1), order_b
    )
    mixing_b = middle_b[:, :width]
    output_w = middle_b[:, width:]
    expand_w = gather_weight(expand_weight, order_a)
    reduce_w = gather_weight(reduce_weight, order_b)
    seg_count = tokens.shape[0]
    seg_len = tokens.shape[2]
    row_count = seg_count * seg_len
    gain_one_f = gain_one.astype(float_kind)
    gain_two_f = gain_two.astype(float_kind)
    tok_rows = tokens.reshape(row_count, width)
    memory_rows = tokens[:, 0, seg_len - MEM :, :].reshape(seg_count * MEM, width)
    mem_query = matmul(tok_rows, query_w).astype(bf_type)
    write_keys = matmul(memory_rows, key_w).astype(bf_type)
    write_vals = matmul(memory_rows, value_w).astype(bf_type)
    gate_prob = jax.nn.sigmoid(matmul(memory_rows, gate_w))
    gate_low = gate_prob.astype(bf_type)
    place = lax.axis_index("dp")
    places = lax.axis_size("dp")
    stream = lax.axis_index("narrow")
    keep_flag = 1.0 - resets.astype(float_kind)
    own_keep = lax.dynamic_index_in_dim(keep_flag[:, 0], stream, 0, False)
    packed = jnp.concatenate(
        [
            write_keys,
            write_vals,
            jnp.broadcast_to(gate_low[:, None], (MEM, 64)),
            jnp.broadcast_to(own_keep.astype(bf_type), (MEM, 64)),
        ],
        axis=1,
    )
    all_rows = (
        gather_bits(packed, order_a, dp_bits).reshape((-1, packed.shape[1])).astype(float_kind)
    )
    all_keys = all_rows[:, :key_width]
    all_vals = all_rows[:, key_width : key_width + width]
    all_gates = all_rows[:, key_width + width : key_width + width + 1]
    keeps = all_rows[::MEM, key_width + width + 64]
    index = jnp.arange(places)
    linked = jnp.prod(
        jnp.where(
            (index[None, :] > index[:, None]) & (index[None, :] <= place), keeps[None, :], 1.0
        ),
        axis=1,
    ) * (index < place)
    start_keep = jnp.prod(jnp.where(index <= place, keeps, 1.0))
    row_link = jnp.repeat(linked, MEM)[None, :]
    key_feat = features(all_keys).astype(bf_type)
    scaled_vals = all_vals * all_gates
    query_features = features(mem_query.astype(float_kind)).astype(bf_type)
    row_scores = (
        lax.dot_general(
            query_features, key_feat, (((1,), (1,)), ((), ())), preferred_element_type=float_kind
        )
        * row_link
    )
    state_read = jnp.concatenate(
        [
            lax.dot_general(
                query_features, part, (((1,), (1,)), ((), ())), preferred_element_type=float_kind
            )
            for part in (memory_top, memory_low)
        ],
        axis=1,
    )
    numerator = start_keep * state_read + exact(row_scores, scaled_vals)
    den_sum = start_keep * jnp.sum(
        query_features.astype(float_kind) * normal_own[None, :], axis=1
    ) + jnp.sum(row_scores, axis=1)
    den_total = 1.0 + den_sum
    first_res = tok_rows.astype(float_kind) + numerator / den_total[:, None]
    normed_one, unit_one, inv_one = norm_forward(first_res, gain_one_f)
    normed_one_low = normed_one.astype(bf_type)
    mixed = matmul(normed_one_low, mixing_a)
    queries = mixed[:, :width].astype(bf_type).reshape(seg_count, seg_len, HEADS, HD)
    key_heads = mixed[:, width:].astype(bf_type).reshape(seg_count, seg_len, HEADS, HD)
    head_values = (
        matmul(normed_one_low, mixing_b).astype(bf_type).reshape(seg_count, seg_len, HEADS, HD)
    )
    block_rows = min(seg_len, 512)
    block_count = seg_len // block_rows

    def attend(flat_idx):
        seg_idx = flat_idx // block_count
        row_start = flat_idx % block_count * block_rows
        query_seg = lax.dynamic_index_in_dim(queries, seg_idx, 0, keepdims=False)
        key_seg = lax.dynamic_index_in_dim(key_heads, seg_idx, 0, keepdims=False)
        value_seg = lax.dynamic_index_in_dim(head_values, seg_idx, 0, keepdims=False)
        scores = block_scores(query_seg, key_seg, row_start)
        top_score = jnp.max(scores, axis=-1, keepdims=True)
        raw_weights = jnp.exp(scores - top_score)
        exp_total = jnp.sum(raw_weights, axis=-1, keepdims=True)
        log_total = top_score[..., 0] + jnp.log(exp_total[..., 0])
        probs = (raw_weights / exp_total).astype(bf_type)
        attended_blk = jnp.einsum(
            "hqk,khd->qhd", probs, value_seg, preferred_element_type=float_kind
        ).astype(bf_type)
        return (attended_blk, log_total)

    attended, log_totals = lax.map(attend, jnp.arange(seg_count * block_count, dtype=jnp.int32))
    attended_rows = attended.reshape(row_count, width)
    log_totals = log_totals.reshape(seg_count, block_count, HEADS, block_rows)
    branch = matmul(attended_rows, output_w)
    second_res = first_res + branch
    normed_two, unit_two, inv_two = norm_forward(second_res, gain_two_f)
    normed_two_low = normed_two.astype(bf_type)
    expanded = matmul(normed_two_low, expand_w)
    activated_low = jax.nn.gelu(expanded, approximate=True).astype(bf_type)
    reduced = matmul(activated_low, reduce_w)
    block_out = (second_res + reduced).astype(bf_type).reshape(seg_count, 1, seg_len, width)
    grad_block = cotangent.reshape(row_count, width)
    grad_reduce = scatter_weight(matmul(activated_low.T, grad_block).astype(bf_type), order_b)
    grad_act = matmul(grad_block, reduce_w.T)
    unused, gelu_pull = jax.vjp(lambda inputs: jax.nn.gelu(inputs, approximate=True), expanded)
    grad_expanded = gelu_pull(grad_act)[0].astype(bf_type)
    grad_expand = scatter_weight(matmul(normed_two_low.T, grad_expanded).astype(bf_type), order_a)
    grad_normed_two = matmul(grad_expanded, expand_w.T)
    grad_in_two, grad_gain_two = norm_backward(grad_normed_two, unit_two, inv_two, gain_two_f)
    grad_second = grad_block.astype(float_kind) + grad_in_two
    grad_branch = grad_second.astype(bf_type)
    grad_output = matmul(attended_rows.T, grad_branch).astype(bf_type)
    grad_att = (
        matmul(grad_branch, output_w.T).astype(bf_type).reshape(seg_count, seg_len, HEADS, HD)
    )

    def attend_back(items):
        query_seg, key_seg, value_seg, grad_seg, log_seg = items
        score_scale = query_seg.shape[-1] ** (-0.5)
        scores = block_scores(query_seg, key_seg, 0)
        probs = jnp.exp(scores - log_seg[0][:, :, None])
        grad_value = jnp.einsum(
            "hqk,qhd->khd", probs.astype(bf_type), grad_seg, preferred_element_type=float_kind
        )
        grad_probs = jnp.einsum(
            "qhd,khd->hqk", grad_seg, value_seg, preferred_element_type=float_kind
        )
        grad_scores = (
            probs * (grad_probs - jnp.sum(probs * grad_probs, axis=-1, keepdims=True))
        ).astype(bf_type)
        query_parts = [
            (
                jnp.einsum("hqk,khd->qhd", grad_scores, key_seg, preferred_element_type=float_kind)
                * score_scale
            ).astype(bf_type)
        ]
        grad_key = (
            jnp.einsum("hqk,qhd->khd", grad_scores, query_seg, preferred_element_type=float_kind)
            * score_scale
        )
        return (
            jnp.concatenate(query_parts, axis=0),
            grad_key.astype(bf_type),
            grad_value.astype(bf_type),
        )

    grad_queries, grad_keys, grad_values = lax.map(
        attend_back, (queries, key_heads, head_values, grad_att, log_totals)
    )
    grad_mixed_a = jnp.concatenate(
        [grad_queries.reshape(row_count, width), grad_keys.reshape(row_count, width)], axis=1
    )
    grad_mixed_b = grad_values.reshape(row_count, width)
    grad_middle_a = scatter_weight(
        matmul(normed_one_low.T, grad_mixed_a).astype(bf_type), order_a
    )
    grad_middle_b = scatter_weight(
        jnp.concatenate(
            [matmul(normed_one_low.T, grad_mixed_b).astype(bf_type), grad_output], axis=1
        ),
        order_b,
    )
    grad_normed_one = matmul(grad_mixed_a, mixing_a.T) + matmul(grad_mixed_b, mixing_b.T)
    grad_in_one, grad_gain_one = norm_backward(grad_normed_one, unit_one, inv_one, gain_one_f)
    grad_first = grad_second + grad_in_one
    grad_num = (grad_first / den_total[:, None]).astype(bf_type)
    grad_den = (-jnp.sum(grad_first * numerator, axis=-1) / (den_total * den_total)).astype(bf_type)
    grad_num_f = grad_num.astype(float_kind)
    grad_den_f = grad_den.astype(float_kind)[:, None]
    grad_scores_mem = (exact(grad_num_f, scaled_vals.T) + grad_den_f) * row_link
    grad_feat = start_keep * (
        matmul(grad_num[:, : width // 2], memory_top)
        + matmul(grad_num[:, width // 2 :], memory_low)
        + grad_den_f * normal_own[None, :]
    ) + exact(grad_scores_mem, key_feat.astype(float_kind))
    grad_mq = features_back(mem_query.astype(float_kind), grad_feat)
    grad_key_feat = exact(grad_scores_mem.T, query_features.astype(float_kind))
    grad_rows = jnp.concatenate(
        [features_back(all_keys, grad_key_feat), exact(row_scores.T, grad_num_f)], axis=1
    )
    live = (place >= places - lax.dynamic_index_in_dim(truncation, stream, 0, False)).astype(
        float_kind
    )
    own_rows = live * scatter_bits(
        grad_rows.reshape((2,) * len(dp_bits) + (MEM, grad_rows.shape[1])), order_a[::-1], dp_bits
    )
    grad_wk = own_rows[:, :key_width]
    grad_wv = own_rows[:, key_width:] * gate_low.astype(float_kind)[:, None]
    grad_gate = jnp.sum(own_rows[:, key_width:] * write_vals.astype(float_kind), axis=1)
    grad_mq_low = grad_mq.astype(bf_type)
    grad_wk_low = grad_wk.astype(bf_type)
    grad_wv_low = grad_wv.astype(bf_type)
    grad_logit = grad_gate.astype(bf_type).astype(float_kind) * gate_prob * (1.0 - gate_prob)
    token_rows = grad_first + matmul(grad_mq_low, query_w.T)
    memory_extra = (
        matmul(grad_wk_low, key_w.T)
        + matmul(grad_wv_low, value_w.T)
        + grad_logit[:, None] * gate_w.astype(float_kind)[None, :]
    )
    token_seg = token_rows.reshape(seg_count, seg_len, width)
    token_seg = token_seg.at[:, seg_len - MEM :, :].add(memory_extra.reshape(seg_count, MEM, width))
    token_grad = token_seg.reshape(seg_count, 1, seg_len, width)
    grad_query = matmul(tok_rows.T, grad_mq_low)
    grad_key = matmul(memory_rows.T, grad_wk_low)
    grad_value = scatter_weight(matmul(memory_rows.T, grad_wv_low).astype(bf_type), order_a)
    grad_gate_w = jnp.dot(memory_rows.astype(float_kind).T, grad_logit, precision=exact_mode)
    grad_vectors = jnp.stack([grad_gate_w, grad_gain_one, grad_gain_two], axis=1)
    grad_early = scatter_weight(
        jnp.concatenate([grad_query, grad_key, jnp.pad(grad_vectors, ((0, 0), (0, 125)))], axis=1),
        order_b,
    )
    return (
        block_out,
        token_grad,
        grad_early[:, :key_width],
        grad_early[:, key_width : 2 * key_width],
        grad_value,
        grad_early[:, 2 * key_width],
        grad_early[:, 2 * key_width + 1],
        jnp.concatenate([grad_middle_a, grad_middle_b[:, :width]], axis=1),
        grad_middle_b[:, width:],
        grad_early[:, 2 * key_width + 2],
        grad_expand,
        grad_reduce,
    )


def solution(mesh):
    placed = (
        P("narrow", "dp", None, None),
        P("narrow", "dp", None, None),
        P(None, "dp"),
        P(),
        P(None, None, "narrow"),
        P(None, "narrow"),
        P(("dp", "narrow"), None),
        P(("dp", "narrow"), None),
        P(("dp", "narrow"), None),
        P(("dp", "narrow")),
        P(("dp", "narrow")),
        P(("dp", "narrow"), None),
        P(("dp", "narrow"), None),
        P(("dp", "narrow")),
        P(("dp", "narrow"), None),
        P(("dp", "narrow"), None),
    )
    return jax.shard_map(
        body,
        mesh=mesh,
        in_specs=placed,
        out_specs=(
            P("narrow", "dp", None, None),
            P("narrow", "dp", None, None),
            P(("dp", "narrow"), None),
            P(("dp", "narrow"), None),
            P(("dp", "narrow"), None),
            P(("dp", "narrow")),
            P(("dp", "narrow")),
            P(("dp", "narrow"), None),
            P(("dp", "narrow"), None),
            P(("dp", "narrow")),
            P(("dp", "narrow"), None),
            P(("dp", "narrow"), None),
        ),
        check_vma=False,
    )
```

```python
import functools

import jax
import jax.numpy as jnp
from jax import lax
from jax.experimental import pallas as pl
from jax.experimental.pallas import tpu as pltpu
from jax.sharding import PartitionSpec as P

HEADS = 12
HD = 64
MEM = 16
ORDER = 3


exact_mode = lax.Precision.HIGHEST
ln_eps = 1e-05
masked_score = -1e30
bf_type = jnp.bfloat16
float_kind = jnp.float32


def bits_of(axis):
    count = lax.axis_size(axis)
    bit = 1
    out = []
    while bit < count:
        out.append((axis, bit))
        bit *= 2
    return out[::-1]

def place_bits():
    return bits_of("dp") + bits_of("narrow")

def own_bit(spot):
    axis, bit = spot
    return (lax.axis_index(axis) // bit) % 2

def exchange(values, spot):
    axis, bit = spot
    return lax.ppermute(values, axis, [(i, i ^ bit) for i in range(lax.axis_size(axis))])

def gather_bits(shard, order, all_bits):
    held = []
    whole = shard
    for spot in order:
        other = exchange(whole, spot)
        at = sum(all_bits.index(b) < all_bits.index(spot) for b in held)
        low = own_bit(spot) == 0
        whole = jnp.where(low, jnp.stack([whole, other], at), jnp.stack([other, whole], at))
        held.append(spot)
    return whole

def scatter_step(state):
    whole, held, order = state
    spot = order[0]
    at = held.index(spot)
    mine = own_bit(spot)
    other = exchange(
        lax.dynamic_index_in_dim(whole, 1 - mine, at, False).astype(bf_type), spot
    )
    whole = lax.dynamic_index_in_dim(whole, mine, at, False).astype(float_kind) + other.astype(
        float_kind
    )
    return (whole, [b for b in held if b != spot], order[1:])


def scatter_bits(whole, order, all_bits):
    state = (whole, all_bits, order)
    while state[2]:
        state = scatter_step(state)
    return state[0]


def after(values, *done):
    for one in done:
        edge = one.reshape(-1)[0] if one.ndim == 1 else one[(0,) * one.ndim]
        values = values + (edge.astype(float_kind) * 0.0).astype(values.dtype)
    return values


def flipped(index, step):
    return index + step - 2 * step * ((index // step) % 2)


def mixed_flip(index, mask):
    for step in (1, 2):
        index = flipped(index, step) if mask & step else index
    return index


def gather_kernel(kinds, count, *refs):
    sources, targets = refs[:count], refs[count : 2 * count]
    send_sem, recv_sem, local_sem = refs[2 * count :]
    dp = lax.axis_index("dp")
    z = lax.axis_index("narrow")
    across = {"c": flipped(dp, 1), "x": flipped(dp, 2), "y": flipped(dp, 4)}
    barrier = pltpu.get_barrier_semaphore()
    peers = [(p, z) for p in across.values()] + [(dp, mixed_flip(z, k)) for k in (1, 2, 3)]
    for peer in peers:
        pl.semaphore_signal(
            barrier, inc=1, device_id=peer, device_id_type=pl.DeviceIdType.MESH
        )
    pl.semaphore_wait(barrier, len(peers))
    sent = []
    memory = count - 1

    def target(a, place, zz):
        if a == memory:
            rows = sources[a].shape[1]
            start = pl.multiple_of(place * rows, 16)
            return targets[a].at[zz, pl.ds(start, rows), :]
        return targets[a].at[place * 4 + zz]

    def slot(a, place, zz):
        return recv_sem.at[a, place * 4 + zz]

    def send(a, source, place, zz, peer, when=None):
        copy = pltpu.make_async_remote_copy(
            src_ref=source,
            dst_ref=target(a, place, zz),
            send_sem=send_sem.at[len(sent)],
            recv_sem=slot(a, place, zz),
            device_id=peer,
            device_id_type=pl.DeviceIdType.MESH,
        )
        if when is None:
            copy.start()
        else:
            pl.when(when)(copy.start)
        sent.append((copy, when))

    def arrive(a, place, zz):
        pltpu.make_async_remote_copy(
            src_ref=target(a, place, zz),
            dst_ref=target(a, place, zz),
            send_sem=send_sem.at[0],
            recv_sem=slot(a, place, zz),
            device_id=(dp, z),
            device_id_type=pl.DeviceIdType.MESH,
        ).wait_recv()

    locals_ = []
    for a in range(count):
        source = sources[a].at[z] if a == memory else sources[a]
        copy = pltpu.make_async_copy(source, target(a, dp, z), local_sem.at[a])
        copy.start()
        locals_.append(copy)
    order = [memory] + list(range(memory))
    for k in range(4):
        zz = mixed_flip(z, k)
        for a in order:
            if k == 0:
                source = sources[a].at[z] if a == memory else sources[a]
            else:
                arrive(a, dp, zz)
                source = target(a, dp, zz)
            if a != memory:
                send(a, source, dp, zz, (dp, jnp.minimum(z + 1, 3)), (zz <= z) & (z < 3))
                send(a, source, dp, zz, (dp, jnp.maximum(z - 1, 0)), (zz >= z) & (z > 0))
            elif k == 0:
                for j in (3, 2, 1):
                    other = mixed_flip(z, j)
                    send(a, sources[a].at[other], dp, z, (dp, other))
            for name in ("x", "y", "c"):
                send(a, source, dp, zz, (across[name], z))
    for k in range(4):
        zz = mixed_flip(z, k)
        for a in order:
            kind = kinds[a] if a != memory else k // 2
            for name, other in (("x", "y"), ("y", "x")):
                arrive(a, across[name], zz)
                got = target(a, across[name], zz)
                if kind == (0 if name == "x" else 1):
                    send(a, got, across[name], zz, (across[other], z))
                send(a, got, across[name], zz, (across["c"], z))
    diagonal = flipped(across["x"], 4)
    for k in range(4):
        zz = mixed_flip(z, k)
        for a in order:
            arrive(a, diagonal, zz)
            send(a, target(a, diagonal, zz), diagonal, zz, (across["c"], z))
    for k in range(4):
        zz = mixed_flip(z, k)
        for a in order:
            for place in (across["c"], flipped(across["c"], 2), flipped(across["c"], 4),
                          flipped(flipped(across["c"], 2), 4)):
                arrive(a, place, zz)
    for copy in locals_:
        copy.wait()
    for copy, when in sent:
        if when is None:
            copy.wait_send()
        else:
            pl.when(when)(copy.wait_send)


def gather_all(arrays, kinds):
    count = len(arrays)
    shards = [jax.ShapeDtypeStruct((32,) + a.shape, a.dtype) for a in arrays[:-1]]
    memory = arrays[-1]
    shards.append(
        jax.ShapeDtypeStruct((memory.shape[0], 8 * memory.shape[1], memory.shape[2]), memory.dtype)
    )
    anywhere = pl.BlockSpec(memory_space=pl.ANY)
    return pl.pallas_call(
        functools.partial(gather_kernel, kinds, count),
        out_shape=shards,
        in_specs=[anywhere] * count,
        out_specs=[anywhere] * count,
        scratch_shapes=[
            pltpu.SemaphoreType.DMA((44 * count,)),
            pltpu.SemaphoreType.DMA((count, 32)),
            pltpu.SemaphoreType.DMA((count,)),
        ],
        name="gather_all",
        compiler_params=pltpu.CompilerParams(collective_id=0, has_side_effects=True),
    )(*arrays)


def reduce_kernel(kinds, count, *refs):
    sources, outs = refs[:count], refs[count : 2 * count]
    held, part, diag, side_x, side_y, above, below = (
        refs[(2 + i) * count : (3 + i) * count] for i in range(7)
    )
    send_sem, recv_sem, local_sem = refs[9 * count :]
    dp = lax.axis_index("dp")
    z = lax.axis_index("narrow")
    across = {"c": flipped(dp, 1), "x": flipped(dp, 2), "y": flipped(dp, 4)}
    core = dp % 2
    own = dp // 2
    by_x, by_y = flipped(own, 1), flipped(own, 2)
    diagonal = flipped(by_x, 2)
    barrier = pltpu.get_barrier_semaphore()
    for peer in across.values():
        pl.semaphore_signal(
            barrier, inc=1, device_id=(peer, z), device_id_type=pl.DeviceIdType.MESH
        )
    for k in (1, 2, 3):
        pl.semaphore_signal(
            barrier, inc=1, device_id=(dp, mixed_flip(z, k)), device_id_type=pl.DeviceIdType.MESH
        )
    pl.semaphore_wait(barrier, 6)
    sent = []

    def copy_of(source, target, a, slot, peer, number):
        return pltpu.make_async_remote_copy(
            src_ref=source,
            dst_ref=target,
            send_sem=send_sem.at[number],
            recv_sem=recv_sem.at[a, slot],
            device_id=peer,
            device_id_type=pl.DeviceIdType.MESH,
        )

    def send(source, target, a, slot, peer, when=None):
        copy = copy_of(source, target, a, slot, peer, len(sent))
        if when is None:
            copy.start()
        else:
            pl.when(when)(copy.start)
        sent.append((copy, when))

    def arrive(target, a, slot):
        copy_of(target, target, a, slot, (dp, z), 0).wait_recv()

    def group(ref, place):
        return ref.at[pl.ds(place * 4, 4)]

    def add(a, target, start, other, other_start, shards):
        rows, cols = target.shape[1:]
        step_rows = rows if rows <= 32 else 32
        step_cols = cols if cols <= 1024 else 768
        col_steps = cols // step_cols
        steps = rows // step_rows * col_steps

        def one(i, carry):
            shard = i // steps
            row = pl.multiple_of((i % steps) // col_steps * step_rows, 8)
            col = pl.multiple_of(i % col_steps * step_cols, 128)
            at = (start + shard, pl.ds(row, step_rows), pl.ds(col, step_cols))
            other_at = (other_start + shard,) + at[1:]
            target[at] = (
                target[at].astype(float_kind) + other[other_at].astype(float_kind)
            ).astype(target.dtype)
            return carry

        lax.fori_loop(0, shards * steps, one, 0)

    loads = {}
    for place_name, place in (("d", diagonal), ("x", by_x), ("y", by_y), ("o", own)):
        for a in range(count):
            theirs = pl.ds((place * 2 + 1 - core) * 4, 4)
            ours = pl.ds((place * 2 + core) * 4, 4)
            send(
                sources[a].at[theirs], group(part[a], place), a, place, (across["c"], z)
            )
            load = pltpu.make_async_copy(
                sources[a].at[ours], group(held[a], place), local_sem.at[a, place]
            )
            load.start()
            loads[(place_name, a)] = load

    def joined(name, place, a):
        loads[(name, a)].wait()
        arrive(group(part[a], place), a, place)
        add(a, held[a], place * 4, part[a], place * 4, 4)

    to_x, to_y = (across["x"], z), (across["y"], z)
    for a in range(count):
        joined("d", diagonal, a)
        send(group(held[a], diagonal), diag[a], a, 4, to_x if kinds[a] == 0 else to_y)
    for a in range(count):
        if kinds[a] == 0:
            joined("x", by_x, a)
            send(group(held[a], by_x), side_x[a], a, 5, to_x)
        else:
            joined("y", by_y, a)
            send(group(held[a], by_y), side_y[a], a, 6, to_y)
    for a in range(count):
        if kinds[a] == 0:
            joined("y", by_y, a)
            arrive(diag[a], a, 4)
            add(a, held[a], by_y * 4, diag[a], 0, 4)
            send(group(held[a], by_y), side_y[a], a, 6, to_y)
        else:
            joined("x", by_x, a)
            arrive(diag[a], a, 4)
            add(a, held[a], by_x * 4, diag[a], 0, 4)
            send(group(held[a], by_x), side_x[a], a, 5, to_x)
    for a in range(count):
        joined("o", own, a)

    def from_below(a, zz):
        arrive(below[a].at[zz], a, 8 + zz)
        add(a, held[a], own * 4 + zz, below[a], zz, 1)

    def from_above(a, zz):
        arrive(above[a].at[zz], a, 12 + zz)
        add(a, held[a], own * 4 + zz, above[a], zz, 1)

    def pass_on(a, far):
        up, down = jnp.minimum(z + far, 3), jnp.maximum(z - far, 0)
        pl.when((z + far <= 3) & (z > 0))(lambda: from_below(a, up))
        send(
            held[a].at[own * 4 + up], below[a].at[up], a, 8 + up,
            (dp, jnp.minimum(z + 1, 3)), z + far <= 3,
        )
        pl.when((z - far >= 0) & (z < 3))(lambda: from_above(a, down))
        send(
            held[a].at[own * 4 + down], above[a].at[down], a, 12 + down,
            (dp, jnp.maximum(z - 1, 0)), z - far >= 0,
        )

    def finish(a):
        pl.when(z > 0)(lambda: from_below(a, z))
        pl.when(z < 3)(lambda: from_above(a, z))
        outs[a][...] = held[a][own * 4 + z].astype(float_kind)

    for turn in range(count + 3):
        for lag in range(4):
            a = turn - lag
            if a < 0 or a >= count:
                continue
            if lag == 0:
                for side, slot in ((side_x, 5), (side_y, 6)):
                    arrive(side[a], a, slot)
                    add(a, held[a], own * 4, side[a], 0, 4)
            if lag < 3:
                pass_on(a, 3 - lag)
            else:
                finish(a)
    for copy, when in sent:
        if when is None:
            copy.wait_send()
        else:
            pl.when(when)(copy.wait_send)


def reduce_all(arrays, kinds):
    count = len(arrays)
    arrays = [a.reshape((32, a.shape[0] // 32, a.shape[1])) for a in arrays]

    def slots(number):
        return [pltpu.VMEM((number,) + a.shape[1:], a.dtype) for a in arrays]

    return pl.pallas_call(
        functools.partial(reduce_kernel, kinds, count),
        out_shape=[jax.ShapeDtypeStruct(a.shape[1:], float_kind) for a in arrays],
        in_specs=[pl.BlockSpec(memory_space=pl.ANY)] * count,
        out_specs=[pl.BlockSpec(memory_space=pltpu.VMEM)] * count,
        scratch_shapes=slots(16) + slots(16) + slots(4) * 5
        + [
            pltpu.SemaphoreType.DMA((13 * count,)),
            pltpu.SemaphoreType.DMA((count, 16)),
            pltpu.SemaphoreType.DMA((count, 4)),
        ],
        name="reduce_all",
        compiler_params=pltpu.CompilerParams(
            collective_id=1, has_side_effects=True, vmem_limit_bytes=60 * 2**20
        ),
    )(*arrays)


def two_orders():
    inner, outer = bits_of("dp")[-1:], bits_of("dp")[:-1]
    return outer + inner, outer[::-1] + inner


def swap_blocks(blocks, spots):
    for at, spot in enumerate(spots):
        mine = own_bit(spot)
        other = exchange(lax.dynamic_index_in_dim(blocks, 1 - mine, at, False), spot)
        kept = lax.dynamic_index_in_dim(blocks, mine, at, False)
        blocks = jnp.where(mine == 0, jnp.stack([kept, other], at), jnp.stack([other, kept], at))
    return blocks


def gather_weight(shard, order):
    whole = gather_bits(shard, bits_of("narrow") + order, place_bits())
    return whole.reshape((-1, shard.shape[-1]))


def scatter_weight(whole, order):
    spots = place_bits()
    split = whole.reshape((2,) * len(spots) + (whole.shape[0] // 2 ** len(spots), whole.shape[1]))
    return scatter_bits(split, order[::-1] + bits_of("narrow")[::-1], spots)


def matmul(left, right):
    return jnp.dot(left, right, preferred_element_type=float_kind)


def rounded(values):
    return lax.optimization_barrier(values.astype(bf_type)).astype(float_kind)


def halves_of(inputs):
    return jnp.concatenate([jax.nn.relu(inputs), jax.nn.relu(-inputs)], axis=-1)


def features(inputs):
    halves = halves_of(inputs)
    return jnp.concatenate(
        [halves * jnp.roll(halves, shift, axis=-1) for shift in range(1, ORDER + 1)], axis=-1
    )


def features_back(inputs, grad):
    key_width = inputs.shape[-1]
    halves = halves_of(inputs)
    total = jnp.zeros_like(halves)
    for shift in range(1, ORDER + 1):
        part = grad[:, (shift - 1) * 2 * key_width : shift * 2 * key_width]
        total = total + part * jnp.roll(halves, shift, axis=-1)
        total = total + jnp.roll(part * halves, -shift, axis=-1)
    return jnp.where(inputs > 0, total[:, :key_width], 0.0) - jnp.where(
        inputs < 0, total[:, key_width:], 0.0
    )


def exact(left, right):
    return jnp.dot(left, right, precision=exact_mode)


def norm_forward(inputs, gain):
    center = inputs - jnp.mean(inputs, axis=-1, keepdims=True)
    inv_std = lax.rsqrt(jnp.mean(center * center, axis=-1, keepdims=True) + ln_eps)
    unit = center * inv_std
    return (unit * gain, unit, inv_std)


def norm_backward(grad_out, unit, inv_std, gain):
    grad_unit = grad_out * gain
    grad_gain = jnp.sum(grad_out * unit, axis=0)
    grad_in = inv_std * (
        grad_unit
        - jnp.mean(grad_unit, axis=-1, keepdims=True)
        - unit * jnp.mean(grad_unit * unit, axis=-1, keepdims=True)
    )
    return (grad_in, grad_gain)


def block_scores(query_blk, key_seg, row_start):
    raw = jnp.einsum(
        "qhd,khd->hqk", query_blk, key_seg, preferred_element_type=float_kind
    ) * query_blk.shape[-1] ** (-0.5)
    rows_pos = row_start + jnp.arange(query_blk.shape[0])
    cols_pos = jnp.arange(key_seg.shape[0])
    return jnp.where((cols_pos[None, :] <= rows_pos[:, None])[None], raw, masked_score)


def body(
    tokens,
    cotangent,
    resets,
    truncation,
    memory_state,
    normalizer,
    query_weight,
    key_weight,
    value_weight,
    gate_weight,
    first_gain,
    mixing_weight,
    output_weight,
    second_gain,
    expand_weight,
    reduce_weight,
):
    order_a, order_b = two_orders()
    narrow_bits = bits_of("narrow")
    dp_bits = bits_of("dp")
    key_width = query_weight.shape[1]
    width = tokens.shape[3]
    vectors = jnp.stack([gate_weight, first_gain, second_gain], axis=1)
    early_shard = jnp.concatenate(
        [query_weight, key_weight, jnp.pad(vectors, ((0, 0), (0, 125)))], axis=1
    )
    block_rows = width // lax.axis_size("dp")
    rows = lax.dynamic_slice_in_dim(
        memory_state, lax.axis_index("dp") * block_rows, block_rows, 1
    ).astype(bf_type)
    if lax.axis_size("dp") == 8 and lax.axis_size("narrow") == 4:
        gathered = gather_all(
            (
                early_shard,
                value_weight,
                mixing_weight,
                output_weight,
                expand_weight,
                reduce_weight,
                rows,
            ),
            (1, 1, 0, 1, 0, 1),
        )
        early_b, value_w, mixing_w, output_w, expand_w, reduce_w = (
            g.reshape((-1, g.shape[-1])) for g in gathered[:-1]
        )
        memory_parts = gathered[-1]
    else:
        early_b = gather_weight(early_shard, order_b)
        value_w = gather_weight(value_weight, order_a)
        mixing_w = gather_weight(mixing_weight, order_a)
        output_w = gather_weight(output_weight, order_b)
        expand_w = gather_weight(expand_weight, order_a)
        reduce_w = gather_weight(reduce_weight, order_b)
        split = rows.reshape((2,) * len(narrow_bits) + rows.shape[1:])
        swapped = swap_blocks(split, narrow_bits).reshape(rows.shape)
        spread = gather_bits(swapped, order_a, dp_bits).reshape((-1,) + rows.shape)
        memory_parts = jnp.swapaxes(spread, 0, 1).reshape(
            (rows.shape[0], width, rows.shape[2])
        )
    query_w = early_b[:, :key_width]
    key_w = early_b[:, key_width : 2 * key_width]
    gate_w = early_b[:, 2 * key_width]
    gain_one = early_b[:, 2 * key_width + 1]
    gain_two = early_b[:, 2 * key_width + 2]
    stream_count = memory_state.shape[0]
    col_count = memory_state.shape[2]
    normal_split = normalizer.reshape((2,) * len(narrow_bits) + normalizer.shape[1:])
    normal_own = swap_blocks(normal_split, narrow_bits).reshape(-1)
    seg_count = tokens.shape[0]
    seg_len = tokens.shape[2]
    row_count = seg_count * seg_len
    gain_one_f = gain_one.astype(float_kind)
    gain_two_f = gain_two.astype(float_kind)
    tok_rows = tokens.reshape(row_count, width)
    memory_rows = tokens[:, 0, seg_len - MEM :, :].reshape(seg_count * MEM, width)
    mem_query = matmul(tok_rows, query_w).astype(bf_type)
    write_keys = matmul(memory_rows, key_w).astype(bf_type)
    write_vals = matmul(memory_rows, value_w).astype(bf_type)
    gate_prob = jax.nn.sigmoid(matmul(memory_rows, gate_w))
    gate_low = gate_prob.astype(bf_type)
    place = lax.axis_index("dp")
    places = lax.axis_size("dp")
    stream = lax.axis_index("narrow")
    keep_flag = 1.0 - resets.astype(float_kind)
    own_keep = lax.dynamic_index_in_dim(keep_flag[:, 0], stream, 0, False)
    packed = jnp.concatenate(
        [
            write_keys,
            write_vals,
            jnp.broadcast_to(gate_low[:, None], (MEM, 64)),
            jnp.broadcast_to(own_keep.astype(bf_type), (MEM, 64)),
        ],
        axis=1,
    )
    all_rows = (
        gather_bits(packed, order_a, dp_bits).reshape((-1, packed.shape[1])).astype(float_kind)
    )
    all_keys = all_rows[:, :key_width]
    all_vals = all_rows[:, key_width : key_width + width]
    all_gates = all_rows[:, key_width + width : key_width + width + 1]
    keeps = all_rows[::MEM, key_width + width + 64]
    index = jnp.arange(places)
    linked = jnp.prod(
        jnp.where(
            (index[None, :] > index[:, None]) & (index[None, :] <= place), keeps[None, :], 1.0
        ),
        axis=1,
    ) * (index < place)
    start_keep = jnp.prod(jnp.where(index <= place, keeps, 1.0))
    row_link = jnp.repeat(linked, MEM)[None, :]
    key_feat = features(all_keys).astype(bf_type)
    scaled_vals = all_vals * all_gates
    query_features = features(mem_query.astype(float_kind)).astype(bf_type)
    row_scores = (
        lax.dot_general(
            query_features, key_feat, (((1,), (1,)), ((), ())), preferred_element_type=float_kind
        )
        * row_link
    )
    state_read = sum(
        lax.dot_general(
            query_features[:, i * col_count : (i + 1) * col_count],
            memory_parts[i],
            (((1,), (1,)), ((), ())),
            preferred_element_type=float_kind,
        )
        for i in range(stream_count)
    )
    numerator = start_keep * state_read + exact(row_scores, scaled_vals)
    den_sum = start_keep * jnp.sum(
        query_features.astype(float_kind) * normal_own[None, :], axis=1
    ) + jnp.sum(row_scores, axis=1)
    den_total = 1.0 + den_sum
    first_res = tok_rows.astype(float_kind) + numerator / den_total[:, None]
    normed_one, unit_one, inv_one = norm_forward(first_res, gain_one_f)
    normed_one_low = normed_one.astype(bf_type)
    mixed = matmul(normed_one_low, mixing_w)
    queries = mixed[:, :width].astype(bf_type).reshape(seg_count, seg_len, HEADS, HD)
    key_heads = mixed[:, width : 2 * width].astype(bf_type).reshape(seg_count, seg_len, HEADS, HD)
    head_values = mixed[:, 2 * width :].astype(bf_type).reshape(seg_count, seg_len, HEADS, HD)
    block_rows = min(seg_len, 512)
    block_count = seg_len // block_rows

    def attend(flat_idx):
        seg_idx = flat_idx // block_count
        row_start = flat_idx % block_count * block_rows
        query_seg = lax.dynamic_index_in_dim(queries, seg_idx, 0, keepdims=False)
        key_seg = lax.dynamic_index_in_dim(key_heads, seg_idx, 0, keepdims=False)
        value_seg = lax.dynamic_index_in_dim(head_values, seg_idx, 0, keepdims=False)
        scores = block_scores(query_seg, key_seg, row_start)
        top_score = jnp.max(scores, axis=-1, keepdims=True)
        raw_weights = jnp.exp(scores - top_score)
        exp_total = jnp.sum(raw_weights, axis=-1, keepdims=True)
        log_total = top_score[..., 0] + jnp.log(exp_total[..., 0])
        probs = (raw_weights / exp_total).astype(bf_type)
        attended_blk = jnp.einsum(
            "hqk,khd->qhd", probs, value_seg, preferred_element_type=float_kind
        ).astype(bf_type)
        return (attended_blk, log_total)

    attended, log_totals = lax.map(attend, jnp.arange(seg_count * block_count, dtype=jnp.int32))
    attended_rows = attended.reshape(row_count, width)
    log_totals = log_totals.reshape(seg_count, block_count, HEADS, block_rows)
    branch = matmul(attended_rows, output_w)
    second_res = first_res + branch
    normed_two, unit_two, inv_two = norm_forward(second_res, gain_two_f)
    normed_two_low = normed_two.astype(bf_type)
    expanded = matmul(normed_two_low, expand_w)
    activated_low = jax.nn.gelu(expanded, approximate=True).astype(bf_type)
    reduced = matmul(activated_low, reduce_w)
    block_out = (second_res + reduced).astype(bf_type).reshape(seg_count, 1, seg_len, width)
    grad_block = cotangent.reshape(row_count, width)
    grad_reduce = matmul(activated_low.T, grad_block).astype(bf_type)
    grad_act = matmul(grad_block, reduce_w.T)
    unused, gelu_pull = jax.vjp(lambda inputs: jax.nn.gelu(inputs, approximate=True), expanded)
    grad_expanded = gelu_pull(grad_act)[0].astype(bf_type)
    grad_expand = matmul(normed_two_low.T, grad_expanded).astype(bf_type)
    grad_normed_two = matmul(grad_expanded, expand_w.T)
    grad_in_two, grad_gain_two = norm_backward(grad_normed_two, unit_two, inv_two, gain_two_f)
    grad_second = grad_block.astype(float_kind) + grad_in_two
    grad_branch = grad_second.astype(bf_type)
    grad_output = matmul(attended_rows.T, grad_branch).astype(bf_type)
    grad_att = (
        matmul(grad_branch, output_w.T).astype(bf_type).reshape(seg_count, seg_len, HEADS, HD)
    )

    def attend_back(items):
        query_seg, key_seg, value_seg, grad_seg, log_seg = items
        score_scale = query_seg.shape[-1] ** (-0.5)
        scores = block_scores(query_seg, key_seg, 0)
        probs = jnp.exp(scores - log_seg[0][:, :, None])
        grad_value = jnp.einsum(
            "hqk,qhd->khd", probs.astype(bf_type), grad_seg, preferred_element_type=float_kind
        )
        grad_probs = jnp.einsum(
            "qhd,khd->hqk", grad_seg, value_seg, preferred_element_type=float_kind
        )
        grad_scores = (
            probs * (grad_probs - jnp.sum(probs * grad_probs, axis=-1, keepdims=True))
        ).astype(bf_type)
        query_parts = [
            (
                jnp.einsum("hqk,khd->qhd", grad_scores, key_seg, preferred_element_type=float_kind)
                * score_scale
            ).astype(bf_type)
        ]
        grad_key = (
            jnp.einsum("hqk,qhd->khd", grad_scores, query_seg, preferred_element_type=float_kind)
            * score_scale
        )
        return (
            jnp.concatenate(query_parts, axis=0),
            grad_key.astype(bf_type),
            grad_value.astype(bf_type),
        )

    grad_queries, grad_keys, grad_values = lax.map(
        attend_back, (queries, key_heads, head_values, grad_att, log_totals)
    )
    grad_mixed = jnp.concatenate(
        [
            grad_queries.reshape(row_count, width),
            grad_keys.reshape(row_count, width),
            grad_values.reshape(row_count, width),
        ],
        axis=1,
    )
    grad_mixing = matmul(normed_one_low.T, grad_mixed).astype(bf_type)
    grad_normed_one = matmul(grad_mixed, mixing_w.T)
    grad_in_one, grad_gain_one = norm_backward(grad_normed_one, unit_one, inv_one, gain_one_f)
    grad_first = grad_second + grad_in_one
    grad_num = (grad_first / den_total[:, None]).astype(bf_type)
    grad_den = (-jnp.sum(grad_first * numerator, axis=-1) / (den_total * den_total)).astype(bf_type)
    grad_num_f = grad_num.astype(float_kind)
    grad_den_f = grad_den.astype(float_kind)[:, None]
    grad_scores_mem = (exact(grad_num_f, scaled_vals.T) + grad_den_f) * row_link
    grad_feat = start_keep * (
        jnp.concatenate(
            [matmul(grad_num, memory_parts[i]) for i in range(stream_count)], axis=1
        )
        + grad_den_f * normal_own[None, :]
    ) + exact(grad_scores_mem, key_feat.astype(float_kind))
    grad_mq = features_back(mem_query.astype(float_kind), grad_feat)
    grad_key_feat = exact(grad_scores_mem.T, query_features.astype(float_kind))
    grad_rows = jnp.concatenate(
        [features_back(all_keys, grad_key_feat), exact(row_scores.T, grad_num_f)], axis=1
    )
    live = (place >= places - lax.dynamic_index_in_dim(truncation, stream, 0, False)).astype(
        float_kind
    )
    own_rows = live * scatter_bits(
        grad_rows.reshape((2,) * len(dp_bits) + (MEM, grad_rows.shape[1])), order_a[::-1], dp_bits
    )
    grad_wk = own_rows[:, :key_width]
    grad_wv = own_rows[:, key_width:] * gate_low.astype(float_kind)[:, None]
    grad_gate = jnp.sum(own_rows[:, key_width:] * write_vals.astype(float_kind), axis=1)
    grad_mq_low = grad_mq.astype(bf_type)
    grad_wk_low = grad_wk.astype(bf_type)
    grad_wv_low = grad_wv.astype(bf_type)
    grad_logit = grad_gate.astype(bf_type).astype(float_kind) * gate_prob * (1.0 - gate_prob)
    token_rows = grad_first + matmul(grad_mq_low, query_w.T)
    memory_extra = (
        matmul(grad_wk_low, key_w.T)
        + matmul(grad_wv_low, value_w.T)
        + grad_logit[:, None] * gate_w.astype(float_kind)[None, :]
    )
    token_seg = token_rows.reshape(seg_count, seg_len, width)
    token_seg = token_seg.at[:, seg_len - MEM :, :].add(memory_extra.reshape(seg_count, MEM, width))
    token_grad = token_seg.reshape(seg_count, 1, seg_len, width)
    grad_query = matmul(tok_rows.T, grad_mq_low)
    grad_key = matmul(memory_rows.T, grad_wk_low)
    grad_value = matmul(memory_rows.T, grad_wv_low).astype(bf_type)
    grad_gate_w = jnp.dot(memory_rows.astype(float_kind).T, grad_logit, precision=exact_mode)
    grad_vectors = jnp.stack([grad_gate_w, grad_gain_one, grad_gain_two], axis=1)
    grad_early = jnp.concatenate(
        [grad_query, grad_key, jnp.pad(grad_vectors, ((0, 0), (0, 125)))], axis=1
    ).astype(bf_type)
    grads = [grad_reduce, grad_expand, grad_mixing, grad_output, grad_value, grad_early]
    kinds = (1, 0, 0, 1, 1, 1)
    if lax.axis_size("dp") == 8 and lax.axis_size("narrow") == 4:
        grads = reduce_all(grads, kinds)
    else:
        grads = [scatter_weight(g, order_b if k else order_a) for g, k in zip(grads, kinds)]
    grad_reduce, grad_expand, grad_mixing, grad_output, grad_value, grad_early = grads
    return (
        block_out,
        token_grad,
        grad_early[:, :key_width],
        grad_early[:, key_width : 2 * key_width],
        grad_value,
        grad_early[:, 2 * key_width],
        grad_early[:, 2 * key_width + 1],
        grad_mixing,
        grad_output,
        grad_early[:, 2 * key_width + 2],
        grad_expand,
        grad_reduce,
    )


def solution(mesh):
    placed = (
        P("narrow", "dp", None, None),
        P("narrow", "dp", None, None),
        P(None, "dp"),
        P(),
        P(None, None, "narrow"),
        P(None, "narrow"),
        P(("dp", "narrow"), None),
        P(("dp", "narrow"), None),
        P(("dp", "narrow"), None),
        P(("dp", "narrow")),
        P(("dp", "narrow")),
        P(("dp", "narrow"), None),
        P(("dp", "narrow"), None),
        P(("dp", "narrow")),
        P(("dp", "narrow"), None),
        P(("dp", "narrow"), None),
    )
    return jax.shard_map(
        body,
        mesh=mesh,
        in_specs=placed,
        out_specs=(
            P("narrow", "dp", None, None),
            P("narrow", "dp", None, None),
            P(("dp", "narrow"), None),
            P(("dp", "narrow"), None),
            P(("dp", "narrow"), None),
            P(("dp", "narrow")),
            P(("dp", "narrow")),
            P(("dp", "narrow"), None),
            P(("dp", "narrow"), None),
            P(("dp", "narrow")),
            P(("dp", "narrow"), None),
            P(("dp", "narrow"), None),
        ),
        check_vma=False,
    )
```

```python
import functools

import jax
import jax.numpy as jnp
from jax import lax
from jax.experimental import pallas as pl
from jax.experimental.pallas import tpu as pltpu
from jax.sharding import PartitionSpec as P

HEADS = 12
HD = 64
MEM = 16
ORDER = 3


exact_mode = lax.Precision.HIGHEST
ln_eps = 1e-05
masked_score = -1e30
bf_type = jnp.bfloat16
float_kind = jnp.float32


def bits_of(axis):
    count = lax.axis_size(axis)
    bit = 1
    out = []
    while bit < count:
        out.append((axis, bit))
        bit *= 2
    return out[::-1]

def place_bits():
    return bits_of("dp") + bits_of("narrow")

def own_bit(spot):
    axis, bit = spot
    return (lax.axis_index(axis) // bit) % 2

def exchange(values, spot):
    axis, bit = spot
    return lax.ppermute(values, axis, [(i, i ^ bit) for i in range(lax.axis_size(axis))])

def gather_bits(shard, order, all_bits):
    held = []
    whole = shard
    for spot in order:
        other = exchange(whole, spot)
        at = sum(all_bits.index(b) < all_bits.index(spot) for b in held)
        low = own_bit(spot) == 0
        whole = jnp.where(low, jnp.stack([whole, other], at), jnp.stack([other, whole], at))
        held.append(spot)
    return whole

def scatter_step(state):
    whole, held, order = state
    spot = order[0]
    at = held.index(spot)
    mine = own_bit(spot)
    other = exchange(
        lax.dynamic_index_in_dim(whole, 1 - mine, at, False).astype(bf_type), spot
    )
    whole = lax.dynamic_index_in_dim(whole, mine, at, False).astype(float_kind) + other.astype(
        float_kind
    )
    return (whole, [b for b in held if b != spot], order[1:])


def scatter_bits(whole, order, all_bits):
    state = (whole, all_bits, order)
    while state[2]:
        state = scatter_step(state)
    return state[0]


def after(values, *done):
    for one in done:
        edge = one.reshape(-1)[0] if one.ndim == 1 else one[(0,) * one.ndim]
        values = values + (edge.astype(float_kind) * 0.0).astype(values.dtype)
    return values


def flipped(index, step):
    return index + step - 2 * step * ((index // step) % 2)


def mixed_flip(index, mask):
    for step in (1, 2):
        index = flipped(index, step) if mask & step else index
    return index


def gather_kernel(kinds, count, *refs):
    sources, targets = refs[:count], refs[count : 2 * count]
    send_sem, recv_sem, local_sem = refs[2 * count :]
    dp = lax.axis_index("dp")
    z = lax.axis_index("narrow")
    across = {"c": flipped(dp, 1), "x": flipped(dp, 2), "y": flipped(dp, 4)}
    barrier = pltpu.get_barrier_semaphore()
    peers = [(p, z) for p in across.values()] + [(dp, mixed_flip(z, k)) for k in (1, 2, 3)]
    for peer in peers:
        pl.semaphore_signal(
            barrier, inc=1, device_id=peer, device_id_type=pl.DeviceIdType.MESH
        )
    pl.semaphore_wait(barrier, len(peers))
    sent = []
    memory = count - 1

    def target(a, place, zz):
        if a == memory:
            rows = sources[a].shape[1]
            start = pl.multiple_of(place * rows, 16)
            return targets[a].at[zz, pl.ds(start, rows), :]
        return targets[a].at[place * 4 + zz]

    def slot(a, place, zz):
        return recv_sem.at[a, place * 4 + zz]

    def send(a, source, place, zz, peer, when=None):
        copy = pltpu.make_async_remote_copy(
            src_ref=source,
            dst_ref=target(a, place, zz),
            send_sem=send_sem.at[len(sent)],
            recv_sem=slot(a, place, zz),
            device_id=peer,
            device_id_type=pl.DeviceIdType.MESH,
        )
        if when is None:
            copy.start()
        else:
            pl.when(when)(copy.start)
        sent.append((copy, when))

    def arrive(a, place, zz):
        pltpu.make_async_remote_copy(
            src_ref=target(a, place, zz),
            dst_ref=target(a, place, zz),
            send_sem=send_sem.at[0],
            recv_sem=slot(a, place, zz),
            device_id=(dp, z),
            device_id_type=pl.DeviceIdType.MESH,
        ).wait_recv()

    locals_ = []
    for a in range(count):
        source = sources[a].at[z] if a == memory else sources[a]
        copy = pltpu.make_async_copy(source, target(a, dp, z), local_sem.at[a])
        copy.start()
        locals_.append(copy)
    order = [memory] + list(range(memory))
    for k in range(4):
        zz = mixed_flip(z, k)
        for a in order:
            if k == 0:
                source = sources[a].at[z] if a == memory else sources[a]
            else:
                arrive(a, dp, zz)
                source = target(a, dp, zz)
            if a != memory:
                send(a, source, dp, zz, (dp, jnp.minimum(z + 1, 3)), (zz <= z) & (z < 3))
                send(a, source, dp, zz, (dp, jnp.maximum(z - 1, 0)), (zz >= z) & (z > 0))
            elif k == 0:
                for j in (3, 2, 1):
                    other = mixed_flip(z, j)
                    send(a, sources[a].at[other], dp, z, (dp, other))
            for name in ("x", "y", "c"):
                send(a, source, dp, zz, (across[name], z))
    for k in range(4):
        zz = mixed_flip(z, k)
        for a in order:
            kind = kinds[a] if a != memory else k // 2
            for name, other in (("x", "y"), ("y", "x")):
                arrive(a, across[name], zz)
                got = target(a, across[name], zz)
                if kind == (0 if name == "x" else 1):
                    send(a, got, across[name], zz, (across[other], z))
                send(a, got, across[name], zz, (across["c"], z))
    diagonal = flipped(across["x"], 4)
    for k in range(4):
        zz = mixed_flip(z, k)
        for a in order:
            arrive(a, diagonal, zz)
            send(a, target(a, diagonal, zz), diagonal, zz, (across["c"], z))
    for k in range(4):
        zz = mixed_flip(z, k)
        for a in order:
            for place in (across["c"], flipped(across["c"], 2), flipped(across["c"], 4),
                          flipped(flipped(across["c"], 2), 4)):
                arrive(a, place, zz)
    for copy in locals_:
        copy.wait()
    for copy, when in sent:
        if when is None:
            copy.wait_send()
        else:
            pl.when(when)(copy.wait_send)


def gather_all(arrays, kinds):
    count = len(arrays)
    shards = [jax.ShapeDtypeStruct((32,) + a.shape, a.dtype) for a in arrays[:-1]]
    memory = arrays[-1]
    shards.append(
        jax.ShapeDtypeStruct((memory.shape[0], 8 * memory.shape[1], memory.shape[2]), memory.dtype)
    )
    anywhere = pl.BlockSpec(memory_space=pl.ANY)
    return pl.pallas_call(
        functools.partial(gather_kernel, kinds, count),
        out_shape=shards,
        in_specs=[anywhere] * count,
        out_specs=[anywhere] * count,
        scratch_shapes=[
            pltpu.SemaphoreType.DMA((44 * count,)),
            pltpu.SemaphoreType.DMA((count, 32)),
            pltpu.SemaphoreType.DMA((count,)),
        ],
        name="gather_all",
        compiler_params=pltpu.CompilerParams(collective_id=0, has_side_effects=True),
    )(*arrays)


def reduce_kernel(kinds, count, *refs):
    sources, outs = refs[:count], refs[count : 2 * count]
    held, part, diag, side_x, side_y, above, below = (
        refs[(2 + i) * count : (3 + i) * count] for i in range(7)
    )
    send_sem, recv_sem, local_sem = refs[9 * count :]
    dp = lax.axis_index("dp")
    z = lax.axis_index("narrow")
    across = {"c": flipped(dp, 1), "x": flipped(dp, 2), "y": flipped(dp, 4)}
    core = dp % 2
    own = dp // 2
    by_x, by_y = flipped(own, 1), flipped(own, 2)
    diagonal = flipped(by_x, 2)
    barrier = pltpu.get_barrier_semaphore()
    for peer in across.values():
        pl.semaphore_signal(
            barrier, inc=1, device_id=(peer, z), device_id_type=pl.DeviceIdType.MESH
        )
    for k in (1, 2, 3):
        pl.semaphore_signal(
            barrier, inc=1, device_id=(dp, mixed_flip(z, k)), device_id_type=pl.DeviceIdType.MESH
        )
    pl.semaphore_wait(barrier, 6)
    sent = []

    def copy_of(source, target, a, slot, peer, number):
        return pltpu.make_async_remote_copy(
            src_ref=source,
            dst_ref=target,
            send_sem=send_sem.at[number],
            recv_sem=recv_sem.at[a, slot],
            device_id=peer,
            device_id_type=pl.DeviceIdType.MESH,
        )

    def send(source, target, a, slot, peer, when=None):
        copy = copy_of(source, target, a, slot, peer, len(sent))
        if when is None:
            copy.start()
        else:
            pl.when(when)(copy.start)
        sent.append((copy, when))

    def arrive(target, a, slot):
        copy_of(target, target, a, slot, (dp, z), 0).wait_recv()

    def group(ref, place):
        return ref.at[pl.ds(place * 4, 4)]

    def add(a, target, start, other, other_start, shards):
        rows, cols = target.shape[1:]
        step_rows = rows if rows <= 32 else 32
        step_cols = cols if cols <= 1024 else 768
        col_steps = cols // step_cols
        steps = rows // step_rows * col_steps

        def one(i, carry):
            shard = i // steps
            row = pl.multiple_of((i % steps) // col_steps * step_rows, 8)
            col = pl.multiple_of(i % col_steps * step_cols, 128)
            at = (start + shard, pl.ds(row, step_rows), pl.ds(col, step_cols))
            other_at = (other_start + shard,) + at[1:]
            target[at] = (
                target[at].astype(float_kind) + other[other_at].astype(float_kind)
            ).astype(target.dtype)
            return carry

        lax.fori_loop(0, shards * steps, one, 0)

    loads = {}
    for place_name, place in (("d", diagonal), ("x", by_x), ("y", by_y), ("o", own)):
        for a in range(count):
            theirs = pl.ds((place * 2 + 1 - core) * 4, 4)
            ours = pl.ds((place * 2 + core) * 4, 4)
            send(
                sources[a].at[theirs], group(part[a], place), a, place, (across["c"], z)
            )
            load = pltpu.make_async_copy(
                sources[a].at[ours], group(held[a], place), local_sem.at[a, place]
            )
            load.start()
            loads[(place_name, a)] = load

    def joined(name, place, a):
        loads[(name, a)].wait()
        arrive(group(part[a], place), a, place)
        add(a, held[a], place * 4, part[a], place * 4, 4)

    to_x, to_y = (across["x"], z), (across["y"], z)
    for a in range(count):
        joined("d", diagonal, a)
        send(group(held[a], diagonal), diag[a], a, 4, to_x if kinds[a] == 0 else to_y)
    for a in range(count):
        if kinds[a] == 0:
            joined("x", by_x, a)
            send(group(held[a], by_x), side_x[a], a, 5, to_x)
        else:
            joined("y", by_y, a)
            send(group(held[a], by_y), side_y[a], a, 6, to_y)
    for a in range(count):
        if kinds[a] == 0:
            joined("y", by_y, a)
            arrive(diag[a], a, 4)
            add(a, held[a], by_y * 4, diag[a], 0, 4)
            send(group(held[a], by_y), side_y[a], a, 6, to_y)
        else:
            joined("x", by_x, a)
            arrive(diag[a], a, 4)
            add(a, held[a], by_x * 4, diag[a], 0, 4)
            send(group(held[a], by_x), side_x[a], a, 5, to_x)
    for a in range(count):
        joined("o", own, a)

    def from_below(a, zz):
        arrive(below[a].at[zz], a, 8 + zz)
        add(a, held[a], own * 4 + zz, below[a], zz, 1)

    def from_above(a, zz):
        arrive(above[a].at[zz], a, 12 + zz)
        add(a, held[a], own * 4 + zz, above[a], zz, 1)

    def pass_on(a, far):
        up, down = jnp.minimum(z + far, 3), jnp.maximum(z - far, 0)
        pl.when((z + far <= 3) & (z > 0))(lambda: from_below(a, up))
        send(
            held[a].at[own * 4 + up], below[a].at[up], a, 8 + up,
            (dp, jnp.minimum(z + 1, 3)), z + far <= 3,
        )
        pl.when((z - far >= 0) & (z < 3))(lambda: from_above(a, down))
        send(
            held[a].at[own * 4 + down], above[a].at[down], a, 12 + down,
            (dp, jnp.maximum(z - 1, 0)), z - far >= 0,
        )

    def finish(a):
        pl.when(z > 0)(lambda: from_below(a, z))
        pl.when(z < 3)(lambda: from_above(a, z))
        outs[a][...] = held[a][own * 4 + z].astype(float_kind)

    for turn in range(count + 3):
        for lag in range(4):
            a = turn - lag
            if a < 0 or a >= count:
                continue
            if lag == 0:
                for side, slot in ((side_x, 5), (side_y, 6)):
                    arrive(side[a], a, slot)
                    add(a, held[a], own * 4, side[a], 0, 4)
            if lag < 3:
                pass_on(a, 3 - lag)
            else:
                finish(a)
    for copy, when in sent:
        if when is None:
            copy.wait_send()
        else:
            pl.when(when)(copy.wait_send)


def reduce_all(arrays, kinds):
    count = len(arrays)
    arrays = [a.reshape((32, a.shape[0] // 32, a.shape[1])) for a in arrays]

    def slots(number):
        return [pltpu.VMEM((number,) + a.shape[1:], a.dtype) for a in arrays]

    return pl.pallas_call(
        functools.partial(reduce_kernel, kinds, count),
        out_shape=[jax.ShapeDtypeStruct(a.shape[1:], float_kind) for a in arrays],
        in_specs=[pl.BlockSpec(memory_space=pl.ANY)] * count,
        out_specs=[pl.BlockSpec(memory_space=pltpu.VMEM)] * count,
        scratch_shapes=slots(16) + slots(16) + slots(4) * 5
        + [
            pltpu.SemaphoreType.DMA((13 * count,)),
            pltpu.SemaphoreType.DMA((count, 16)),
            pltpu.SemaphoreType.DMA((count, 4)),
        ],
        name="reduce_all",
        compiler_params=pltpu.CompilerParams(
            collective_id=1, has_side_effects=True, vmem_limit_bytes=60 * 2**20
        ),
    )(*arrays)


def two_orders():
    inner, outer = bits_of("dp")[-1:], bits_of("dp")[:-1]
    return outer + inner, outer[::-1] + inner


def swap_blocks(blocks, spots):
    for at, spot in enumerate(spots):
        mine = own_bit(spot)
        other = exchange(lax.dynamic_index_in_dim(blocks, 1 - mine, at, False), spot)
        kept = lax.dynamic_index_in_dim(blocks, mine, at, False)
        blocks = jnp.where(mine == 0, jnp.stack([kept, other], at), jnp.stack([other, kept], at))
    return blocks


def gather_weight(shard, order):
    whole = gather_bits(shard, bits_of("narrow") + order, place_bits())
    return whole.reshape((-1, shard.shape[-1]))


def scatter_weight(whole, order):
    spots = place_bits()
    split = whole.reshape((2,) * len(spots) + (whole.shape[0] // 2 ** len(spots), whole.shape[1]))
    return scatter_bits(split, order[::-1] + bits_of("narrow")[::-1], spots)


def matmul(left, right):
    return jnp.dot(left, right, preferred_element_type=float_kind)


def rounded(values):
    return lax.optimization_barrier(values.astype(bf_type)).astype(float_kind)


def halves_of(inputs):
    return jnp.concatenate([jax.nn.relu(inputs), jax.nn.relu(-inputs)], axis=-1)


def features(inputs):
    halves = halves_of(inputs)
    return jnp.concatenate(
        [halves * jnp.roll(halves, shift, axis=-1) for shift in range(1, ORDER + 1)], axis=-1
    )


def features_back(inputs, grad):
    key_width = inputs.shape[-1]
    halves = halves_of(inputs)
    total = jnp.zeros_like(halves)
    for shift in range(1, ORDER + 1):
        part = grad[:, (shift - 1) * 2 * key_width : shift * 2 * key_width]
        total = total + part * jnp.roll(halves, shift, axis=-1)
        total = total + jnp.roll(part * halves, -shift, axis=-1)
    return jnp.where(inputs > 0, total[:, :key_width], 0.0) - jnp.where(
        inputs < 0, total[:, key_width:], 0.0
    )


def norm_forward(inputs, gain):
    center = inputs - jnp.mean(inputs, axis=-1, keepdims=True)
    inv_std = lax.rsqrt(jnp.mean(center * center, axis=-1, keepdims=True) + ln_eps)
    unit = center * inv_std
    return (unit * gain, unit, inv_std)


def norm_backward(grad_out, unit, inv_std, gain):
    grad_unit = grad_out * gain
    grad_gain = jnp.sum(grad_out * unit, axis=0)
    grad_in = inv_std * (
        grad_unit
        - jnp.mean(grad_unit, axis=-1, keepdims=True)
        - unit * jnp.mean(grad_unit * unit, axis=-1, keepdims=True)
    )
    return (grad_in, grad_gain)


def body(
    tokens,
    cotangent,
    resets,
    truncation,
    memory_state,
    normalizer,
    query_weight,
    key_weight,
    value_weight,
    gate_weight,
    first_gain,
    mixing_weight,
    output_weight,
    second_gain,
    expand_weight,
    reduce_weight,
):
    order_a, order_b = two_orders()
    narrow_bits = bits_of("narrow")
    dp_bits = bits_of("dp")
    key_width = query_weight.shape[1]
    width = tokens.shape[3]
    vectors = jnp.stack([gate_weight, first_gain, second_gain], axis=1)
    early_shard = jnp.concatenate(
        [query_weight, key_weight, jnp.pad(vectors, ((0, 0), (0, 125)))], axis=1
    )
    block_rows = width // lax.axis_size("dp")
    rows = lax.dynamic_slice_in_dim(
        memory_state, lax.axis_index("dp") * block_rows, block_rows, 1
    ).astype(bf_type)
    if lax.axis_size("dp") == 8 and lax.axis_size("narrow") == 4:
        gathered = gather_all(
            (
                early_shard,
                value_weight,
                mixing_weight,
                output_weight,
                expand_weight,
                reduce_weight,
                rows,
            ),
            (1, 1, 0, 1, 0, 1),
        )
        early_b, value_w, mixing_w, output_w, expand_w, reduce_w = (
            g.reshape((-1, g.shape[-1])) for g in gathered[:-1]
        )
        memory_parts = gathered[-1]
    else:
        early_b = gather_weight(early_shard, order_b)
        value_w = gather_weight(value_weight, order_a)
        mixing_w = gather_weight(mixing_weight, order_a)
        output_w = gather_weight(output_weight, order_b)
        expand_w = gather_weight(expand_weight, order_a)
        reduce_w = gather_weight(reduce_weight, order_b)
        split = rows.reshape((2,) * len(narrow_bits) + rows.shape[1:])
        swapped = swap_blocks(split, narrow_bits).reshape(rows.shape)
        spread = gather_bits(swapped, order_a, dp_bits).reshape((-1,) + rows.shape)
        memory_parts = jnp.swapaxes(spread, 0, 1).reshape(
            (rows.shape[0], width, rows.shape[2])
        )
    query_w = early_b[:, :key_width]
    key_w = early_b[:, key_width : 2 * key_width]
    gate_w = early_b[:, 2 * key_width]
    gain_one = early_b[:, 2 * key_width + 1]
    gain_two = early_b[:, 2 * key_width + 2]
    stream_count = memory_state.shape[0]
    col_count = memory_state.shape[2]
    normal_split = normalizer.reshape((2,) * len(narrow_bits) + normalizer.shape[1:])
    normal_own = swap_blocks(normal_split, narrow_bits).reshape(-1)
    seg_count = tokens.shape[0]
    seg_len = tokens.shape[2]
    row_count = seg_count * seg_len
    gain_one_f = gain_one.astype(float_kind)
    gain_two_f = gain_two.astype(float_kind)
    tok_rows = tokens.reshape(row_count, width)
    memory_rows = tokens[:, 0, seg_len - MEM :, :].reshape(seg_count * MEM, width)
    mem_query, query_features, state_read, state_den = read_all(
        tok_rows, early_b, memory_parts, normal_own[None, :], key_width
    )
    write_keys = matmul(memory_rows, key_w).astype(bf_type)
    write_vals = matmul(memory_rows, value_w).astype(bf_type)
    gate_prob = jax.nn.sigmoid(matmul(memory_rows, gate_w))
    gate_low = gate_prob.astype(bf_type)
    place = lax.axis_index("dp")
    places = lax.axis_size("dp")
    stream = lax.axis_index("narrow")
    keep_flag = 1.0 - resets.astype(float_kind)
    own_keep = lax.dynamic_index_in_dim(keep_flag[:, 0], stream, 0, False)
    packed = jnp.concatenate(
        [
            write_keys,
            write_vals,
            jnp.broadcast_to(gate_low[:, None], (MEM, 64)),
            jnp.broadcast_to(own_keep.astype(bf_type), (MEM, 64)),
        ],
        axis=1,
    )
    all_rows = (
        gather_bits(packed, order_a, dp_bits).reshape((-1, packed.shape[1])).astype(float_kind)
    )
    all_keys = all_rows[:, :key_width]
    all_vals = all_rows[:, key_width : key_width + width]
    all_gates = all_rows[:, key_width + width : key_width + width + 1]
    keeps = all_rows[::MEM, key_width + width + 64]
    index = jnp.arange(places)
    linked = jnp.prod(
        jnp.where(
            (index[None, :] > index[:, None]) & (index[None, :] <= place), keeps[None, :], 1.0
        ),
        axis=1,
    ) * (index < place)
    start_keep = jnp.prod(jnp.where(index <= place, keeps, 1.0))
    row_link = jnp.repeat(linked, MEM)[None, :]
    key_feat = features(all_keys).astype(bf_type)
    scaled_vals = all_vals * all_gates
    row_scores = (
        lax.dot_general(
            query_features, key_feat, (((1,), (1,)), ((), ())), preferred_element_type=float_kind
        )
        * row_link
    )
    numerator = start_keep * state_read + jnp.dot(
        row_scores, scaled_vals, precision=lax.Precision.HIGH
    )
    den_sum = start_keep * state_den[:, 0] + jnp.sum(row_scores, axis=1)
    den_total = 1.0 + den_sum
    first_res = tok_rows.astype(float_kind) + numerator / den_total[:, None]
    normed_one, unit_one, inv_one = norm_forward(first_res, gain_one_f)
    normed_one_low = normed_one.astype(bf_type)
    mixed = matmul(normed_one_low, mixing_w).astype(bf_type)
    attended_rows = attend_all(mixed)
    branch = matmul(attended_rows, output_w)
    second_res = first_res + branch
    normed_two, unit_two, inv_two = norm_forward(second_res, gain_two_f)
    normed_two_low = normed_two.astype(bf_type)
    expanded = matmul(normed_two_low, expand_w)
    activated_low = jax.nn.gelu(expanded, approximate=True).astype(bf_type)
    reduced = matmul(activated_low, reduce_w)
    block_out = (second_res + reduced).astype(bf_type).reshape(seg_count, 1, seg_len, width)
    grad_block = cotangent.reshape(row_count, width)
    grad_reduce = matmul(activated_low.T, grad_block).astype(bf_type)
    grad_act = matmul(grad_block, reduce_w.T)
    unused, gelu_pull = jax.vjp(lambda inputs: jax.nn.gelu(inputs, approximate=True), expanded)
    grad_expanded = gelu_pull(grad_act)[0].astype(bf_type)
    grad_expand = matmul(normed_two_low.T, grad_expanded).astype(bf_type)
    grad_normed_two = matmul(grad_expanded, expand_w.T)
    grad_in_two, grad_gain_two = norm_backward(grad_normed_two, unit_two, inv_two, gain_two_f)
    grad_second = grad_block.astype(float_kind) + grad_in_two
    grad_branch = grad_second.astype(bf_type)
    grad_output = matmul(attended_rows.T, grad_branch).astype(bf_type)
    grad_att = matmul(grad_branch, output_w.T).astype(bf_type)
    grad_mixed = attend_back_all(mixed, grad_att)
    grad_mixing = matmul(normed_one_low.T, grad_mixed).astype(bf_type)
    grad_normed_one = matmul(grad_mixed, mixing_w.T)
    grad_in_one, grad_gain_one = norm_backward(grad_normed_one, unit_one, inv_one, gain_one_f)
    grad_first = grad_second + grad_in_one
    grad_num = (grad_first / den_total[:, None]).astype(bf_type)
    grad_den = (-jnp.sum(grad_first * numerator, axis=-1) / (den_total * den_total)).astype(bf_type)
    grad_den_f = grad_den.astype(float_kind)[:, None]
    vals_high, vals_low = split_low(scaled_vals)
    grad_scores_mem = (
        matmul(grad_num, vals_high.T) + matmul(grad_num, vals_low.T) + grad_den_f
    ) * row_link
    grad_mq = read_back_all(
        grad_num,
        jnp.broadcast_to(grad_den_f, (row_count, 128)),
        grad_scores_mem,
        mem_query,
        key_feat,
        memory_parts,
        normal_own[None, :],
        jnp.broadcast_to(start_keep, (1, 128)),
    )
    scores_high, scores_low = split_low(grad_scores_mem)
    grad_key_feat = matmul(scores_high.T, query_features) + matmul(scores_low.T, query_features)
    read_high, read_low = split_low(row_scores)
    grad_rows = jnp.concatenate(
        [
            features_back(all_keys, grad_key_feat),
            matmul(read_high.T, grad_num) + matmul(read_low.T, grad_num),
        ],
        axis=1,
    )
    live = (place >= places - lax.dynamic_index_in_dim(truncation, stream, 0, False)).astype(
        float_kind
    )
    own_rows = live * scatter_bits(
        grad_rows.reshape((2,) * len(dp_bits) + (MEM, grad_rows.shape[1])), order_a[::-1], dp_bits
    )
    grad_wk = own_rows[:, :key_width]
    grad_wv = own_rows[:, key_width:] * gate_low.astype(float_kind)[:, None]
    grad_gate = jnp.sum(own_rows[:, key_width:] * write_vals.astype(float_kind), axis=1)
    grad_mq_low = grad_mq.astype(bf_type)
    grad_wk_low = grad_wk.astype(bf_type)
    grad_wv_low = grad_wv.astype(bf_type)
    grad_logit = grad_gate.astype(bf_type).astype(float_kind) * gate_prob * (1.0 - gate_prob)
    token_rows = grad_first + matmul(grad_mq_low, query_w.T)
    memory_extra = (
        matmul(grad_wk_low, key_w.T)
        + matmul(grad_wv_low, value_w.T)
        + grad_logit[:, None] * gate_w.astype(float_kind)[None, :]
    )
    token_seg = token_rows.reshape(seg_count, seg_len, width)
    token_seg = token_seg.at[:, seg_len - MEM :, :].add(memory_extra.reshape(seg_count, MEM, width))
    token_grad = token_seg.reshape(seg_count, 1, seg_len, width)
    grad_query = matmul(tok_rows.T, grad_mq_low)
    grad_key = matmul(memory_rows.T, grad_wk_low)
    grad_value = matmul(memory_rows.T, grad_wv_low).astype(bf_type)
    grad_gate_w = jnp.dot(memory_rows.astype(float_kind).T, grad_logit, precision=exact_mode)
    grad_vectors = jnp.stack([grad_gate_w, grad_gain_one, grad_gain_two], axis=1)
    grad_early = jnp.concatenate(
        [grad_query, grad_key, jnp.pad(grad_vectors, ((0, 0), (0, 125)))], axis=1
    ).astype(bf_type)
    grads = [grad_reduce, grad_expand, grad_mixing, grad_output, grad_value, grad_early]
    kinds = (1, 0, 0, 1, 1, 1)
    if lax.axis_size("dp") == 8 and lax.axis_size("narrow") == 4:
        grads = reduce_all(grads, kinds)
    else:
        grads = [scatter_weight(g, order_b if k else order_a) for g, k in zip(grads, kinds)]
    grad_reduce, grad_expand, grad_mixing, grad_output, grad_value, grad_early = grads
    return (
        block_out,
        token_grad,
        grad_early[:, :key_width],
        grad_early[:, key_width : 2 * key_width],
        grad_value,
        grad_early[:, 2 * key_width],
        grad_early[:, 2 * key_width + 1],
        grad_mixing,
        grad_output,
        grad_early[:, 2 * key_width + 2],
        grad_expand,
        grad_reduce,
    )


def causal_softmax(query, key, row_start):
    raw = lax.dot_general(
        query, key, (((1,), (1,)), ((), ())), preferred_element_type=float_kind
    ) * (HD ** (-0.5))
    rows = lax.broadcasted_iota(jnp.int32, raw.shape, 0) + row_start
    cols = lax.broadcasted_iota(jnp.int32, raw.shape, 1)
    raw = jnp.where(cols <= rows, raw, masked_score)
    weights = jnp.exp(raw - jnp.max(raw, axis=1, keepdims=True))
    return weights / jnp.sum(weights, axis=1, keepdims=True)


def attend_kernel(q_ref, k_ref, v_ref, o_ref):
    seg_len = q_ref.shape[0]
    half = seg_len // 2
    for part in range(2):
        rows = slice(part * half, (part + 1) * half)
        keys = slice(0, (part + 1) * half)
        pieces = []
        for head in range(q_ref.shape[1] // HD):
            lanes = slice(head * HD, (head + 1) * HD)
            probs = causal_softmax(q_ref[rows, lanes], k_ref[keys, lanes], part * half)
            pieces.append(
                jnp.dot(
                    probs.astype(bf_type), v_ref[keys, lanes], preferred_element_type=float_kind
                )
            )
        o_ref[rows, :] = jnp.concatenate(pieces, axis=1).astype(bf_type)


def attend_back_kernel(q_ref, k_ref, v_ref, g_ref, o_ref):
    seg_len, pair = q_ref.shape
    width = o_ref.shape[1] // 3
    half = seg_len // 2
    start = pl.multiple_of(pl.program_id(0) * pair, pair)
    scale = HD ** (-0.5)
    tall = (((0,), (0,)), ((), ()))
    grads_q, grads_k, grads_v = [[], []], [], []
    for head in range(pair // HD):
        lanes = slice(head * HD, (head + 1) * HD)
        key_parts, value_parts = [], []
        for part in range(2):
            rows = slice(part * half, (part + 1) * half)
            keys = slice(0, (part + 1) * half)
            query, grad = q_ref[rows, lanes], g_ref[rows, lanes]
            key, value = k_ref[keys, lanes], v_ref[keys, lanes]
            probs = causal_softmax(query, key, part * half)
            grad_probs = lax.dot_general(
                grad, value, (((1,), (1,)), ((), ())), preferred_element_type=float_kind
            )
            weighted = probs * grad_probs
            grad_scores = (
                weighted - probs * jnp.sum(weighted, axis=1, keepdims=True)
            ).astype(bf_type)
            grads_q[part].append(
                jnp.dot(grad_scores, key, preferred_element_type=float_kind) * scale
            )
            key_parts.append(
                lax.dot_general(grad_scores, query, tall, preferred_element_type=float_kind)
            )
            value_parts.append(
                lax.dot_general(
                    probs.astype(bf_type), grad, tall, preferred_element_type=float_kind
                )
            )
        for kept, parts, by in ((grads_k, key_parts, scale), (grads_v, value_parts, 1.0)):
            top = (parts[0] + parts[1][:half]) * by
            kept.append(jnp.concatenate([top, parts[1][half:] * by], axis=0))
    for part in range(2):
        o_ref[part * half : (part + 1) * half, pl.ds(start, pair)] = jnp.concatenate(
            grads_q[part], axis=1
        ).astype(bf_type)
    for place, kept in ((1, grads_k), (2, grads_v)):
        o_ref[:, pl.ds(place * width + start, pair)] = jnp.concatenate(kept, axis=1).astype(
            bf_type
        )


def attend_all(mixed):
    seg_len, width = mixed.shape[0], mixed.shape[1] // 3
    pair = 2 * HD
    count = width // pair
    specs = [
        pl.BlockSpec((seg_len, pair), functools.partial(lambda j, i: (0, j * count + i), j))
        for j in range(3)
    ]
    return pl.pallas_call(
        attend_kernel,
        grid=(count,),
        out_shape=jax.ShapeDtypeStruct((seg_len, width), bf_type),
        in_specs=specs,
        out_specs=pl.BlockSpec((seg_len, pair), lambda i: (0, i)),
        name="attend",
        compiler_params=pltpu.CompilerParams(vmem_limit_bytes=48 * 2**20),
    )(mixed, mixed, mixed)


def attend_back_all(mixed, grad):
    seg_len, width = grad.shape
    pair = 2 * HD
    count = width // pair
    specs = [
        pl.BlockSpec((seg_len, pair), functools.partial(lambda j, i: (0, j * count + i), j))
        for j in (0, 1, 2, 0)
    ]
    return pl.pallas_call(
        attend_back_kernel,
        grid=(count,),
        out_shape=jax.ShapeDtypeStruct(mixed.shape, bf_type),
        in_specs=specs,
        out_specs=pl.BlockSpec(mixed.shape, lambda i: (0, 0)),
        name="attend_back",
        compiler_params=pltpu.CompilerParams(vmem_limit_bytes=48 * 2**20),
    )(mixed, mixed, mixed, grad)


def split_low(values):
    high = lax.reduce_precision(values, 8, 7)
    return high.astype(bf_type), (values - high).astype(bf_type)


def read_kernel(x_ref, w_ref, mem_ref, norm_ref, mq_ref, qf_ref, num_ref, den_ref):
    key_width = mq_ref.shape[1]
    mem_query = jnp.dot(
        x_ref[...], w_ref[:, :key_width], preferred_element_type=float_kind
    ).astype(bf_type)
    mq_ref[...] = mem_query
    inputs = mem_query.astype(float_kind)
    halves = jnp.concatenate([jnp.maximum(inputs, 0.0), jnp.maximum(-inputs, 0.0)], axis=1)
    den = jnp.zeros((inputs.shape[0], 1), float_kind)
    for i in range(ORDER):
        cols = slice(i * 2 * key_width, (i + 1) * 2 * key_width)
        feat = (halves * pltpu.roll(halves, i + 1, 1)).astype(bf_type)
        qf_ref[:, cols] = feat
        den = den + jnp.sum(
            feat.astype(float_kind) * norm_ref[:, cols], axis=1, keepdims=True
        )
    den_ref[...] = jnp.broadcast_to(den, den_ref.shape)
    total = jnp.zeros(num_ref.shape, float_kind)
    count, _, col_count = mem_ref.shape
    for i in range(count):
        total = total + lax.dot_general(
            qf_ref[:, i * col_count : (i + 1) * col_count],
            mem_ref[i],
            (((1,), (1,)), ((), ())),
            preferred_element_type=float_kind,
        )
    num_ref[...] = total


def row_blocks(rows):
    block = 256 if rows % 256 == 0 else rows
    whole = lambda a: pl.BlockSpec(a.shape, lambda i: (0,) * a.ndim)
    part = lambda cols: pl.BlockSpec((block, cols), lambda i: (i, 0))
    return rows // block, whole, part


def read_all(x, weight, memory, norm, key_width):
    rows, width = x.shape
    features_count = norm.shape[1]
    grid, whole, part = row_blocks(rows)
    return pl.pallas_call(
        read_kernel,
        grid=(grid,),
        out_shape=[
            jax.ShapeDtypeStruct((rows, key_width), bf_type),
            jax.ShapeDtypeStruct((rows, features_count), bf_type),
            jax.ShapeDtypeStruct((rows, width), float_kind),
            jax.ShapeDtypeStruct((rows, 128), float_kind),
        ],
        in_specs=[part(width), whole(weight), whole(memory), whole(norm)],
        out_specs=[part(key_width), part(features_count), part(width), part(128)],
        name="memory_read",
        cost_estimate=pl.CostEstimate(flops=2 * 10**9, bytes_accessed=10**7, transcendentals=0),
        compiler_params=pltpu.CompilerParams(vmem_limit_bytes=48 * 2**20),
    )(x, weight, memory, norm)


def read_back_kernel(
    gnum_ref, gden_ref, gs_ref, mq_ref, kf_ref, mem_ref, norm_ref, keep_ref, out_ref, grad_ref
):
    key_width = mq_ref.shape[1]
    count, _, col_count = mem_ref.shape
    keep = keep_ref[:, :1]
    for i in range(count):
        grad_ref[:, i * col_count : (i + 1) * col_count] = jnp.dot(
            gnum_ref[...], mem_ref[i], preferred_element_type=float_kind
        )
    inputs = mq_ref[...].astype(float_kind)
    halves = jnp.concatenate([jnp.maximum(inputs, 0.0), jnp.maximum(-inputs, 0.0)], axis=1)
    scores = gs_ref[...]
    high = scores.astype(bf_type)
    low = (scores - high.astype(float_kind)).astype(bf_type)
    grad_den = gden_ref[:, :1]
    total = jnp.zeros_like(halves)
    for i in range(ORDER):
        cols = slice(i * 2 * key_width, (i + 1) * 2 * key_width)
        key_feat = kf_ref[:, cols]
        grad = (
            keep * (grad_ref[:, cols] + grad_den * norm_ref[:, cols])
            + jnp.dot(high, key_feat, preferred_element_type=float_kind)
            + jnp.dot(low, key_feat, preferred_element_type=float_kind)
        )
        total = total + grad * pltpu.roll(halves, i + 1, 1)
        total = total + pltpu.roll(grad * halves, 2 * key_width - i - 1, 1)
    out_ref[...] = (
        jnp.where(inputs > 0, total[:, :key_width], 0.0)
        - jnp.where(inputs < 0, total[:, key_width:], 0.0)
    ).astype(bf_type)


def read_back_all(grad_num, grad_den, scores, mem_query, key_feat, memory, norm, keep):
    rows = grad_num.shape[0]
    grid, whole, part = row_blocks(rows)
    block = rows // grid
    return pl.pallas_call(
        read_back_kernel,
        grid=(grid,),
        out_shape=jax.ShapeDtypeStruct(mem_query.shape, bf_type),
        in_specs=[
            part(grad_num.shape[1]),
            part(128),
            part(scores.shape[1]),
            part(mem_query.shape[1]),
            whole(key_feat),
            whole(memory),
            whole(norm),
            whole(keep),
        ],
        out_specs=part(mem_query.shape[1]),
        scratch_shapes=[pltpu.VMEM((block, norm.shape[1]), float_kind)],
        name="memory_read_back",
        cost_estimate=pl.CostEstimate(flops=2 * 10**9, bytes_accessed=10**7, transcendentals=0),
        compiler_params=pltpu.CompilerParams(vmem_limit_bytes=48 * 2**20),
    )(grad_num, grad_den, scores, mem_query, key_feat, memory, norm, keep)


def solution(mesh):
    placed = (
        P("narrow", "dp", None, None),
        P("narrow", "dp", None, None),
        P(None, "dp"),
        P(),
        P(None, None, "narrow"),
        P(None, "narrow"),
        P(("dp", "narrow"), None),
        P(("dp", "narrow"), None),
        P(("dp", "narrow"), None),
        P(("dp", "narrow")),
        P(("dp", "narrow")),
        P(("dp", "narrow"), None),
        P(("dp", "narrow"), None),
        P(("dp", "narrow")),
        P(("dp", "narrow"), None),
        P(("dp", "narrow"), None),
    )
    return jax.shard_map(
        body,
        mesh=mesh,
        in_specs=placed,
        out_specs=(
            P("narrow", "dp", None, None),
            P("narrow", "dp", None, None),
            P(("dp", "narrow"), None),
            P(("dp", "narrow"), None),
            P(("dp", "narrow"), None),
            P(("dp", "narrow")),
            P(("dp", "narrow")),
            P(("dp", "narrow"), None),
            P(("dp", "narrow"), None),
            P(("dp", "narrow")),
            P(("dp", "narrow"), None),
            P(("dp", "narrow"), None),
        ),
        check_vma=False,
    )
```
